128 devices in a mesh: dp: 16 (over x_lo, z, core), seq: 8 (over x_hi, y).
Axes of the slice: x: 4 (x_hi: 2, x_lo: 2; x = x_hi * 2 + x_lo), y: 4, z: 4, core: 2. Of those that a mesh axis runs over, the one named last changes fastest.
Arguments:
- video: bfloat16 [16, 8, 256, 1152], P('dp', 'seq'), may hold values from -6 to 6
- out_grad: bfloat16 [16, 8, 256, 1152], P('dp', 'seq'), may hold values from -6 to 6
- gain_spatial: float32 [1152], replicated, may hold values from 0.1 to 1.9
- gain_temporal: float32 [1152], replicated, may hold values from 0.1 to 1.9
- w_spatial_qkv: bfloat16 [1152, 3456], replicated, may hold values from -4 to 4
- w_spatial_out: bfloat16 [1152, 1152], replicated, may hold values from -0.1875 to 0.1875
- w_temporal_qkv: bfloat16 [1152, 3456], replicated, may hold values from -4 to 4
- w_temporal_out: bfloat16 [1152, 1152], replicated, may hold values from -0.1875 to 0.1875
Outputs:
- video_grad: bfloat16 [16, 8, 256, 1152], P('dp', 'seq')
- w_grad: float32 [1152, 1152], P(('dp', 'seq'))
The draws below stay inside these ranges and needn't reach their ends.
All inputs are finite; a program needn't handle non-finite values.
Results may differ from the reference program's by a relative error of at most 0.018.
Values may be sent and summed in bfloat16 or wider, within the bound.
No kernel may reach another device: no remote copies, remote signals or barrier semaphores. Data moves between devices by JAX's collectives and lax.ppermute only.
A program may use at most 128 MiB of HBM per device.

```python
import math
import jax
import jax.numpy as jnp
from jax import lax

D = 1152
HEADS = 16
P_SIZE = 256
F = 8
VIDEOS = 16


def qkv_table(key):
    normal_table = jax.random.normal(key, (D, 3 * D), jnp.float32) / math.sqrt(D)
    return normal_table.astype(jnp.bfloat16)


def draw_w_spatial_qkv(key, part):
    return qkv_table(jax.random.fold_in(key, 101))


def draw_w_temporal_qkv(key, part):
    return qkv_table(jax.random.fold_in(key, 202))


def level_of(stream_key, shape, shards, smallest, top_value):
    def one(axis_at, parts):
        draws = jax.random.uniform(jax.random.fold_in(jax.random.fold_in(stream_key, 6), axis_at), (parts,), jnp.float32, smallest / len(shards), top_value / len(shards))
        return jnp.repeat(jnp.exp(draws), shape[axis_at] // parts).reshape((-1,) + (1,) * (len(shape) - axis_at - 1))

    factor_of = one(*shards[0])
    for cut in shards[1:]:
        factor_of = factor_of * one(*cut)
    return factor_of


def normal_values(stream_key, dims, scale, most, split=(), dtype=jnp.bfloat16):
    values = jax.random.normal(stream_key, dims, jnp.float32) * scale
    if len(split) > 0:
        values = level_of(stream_key, dims, split, -0.22, 0.18) * values
    return jnp.clip(values, min=-most, max=most).astype(dtype)


def setup_inputs(seed: int = 0) -> dict:
    seeds = jax.random.split(jax.random.key(seed), 9)
    return {
        "video": normal_values(seeds[0], (VIDEOS, F, P_SIZE, D), 1.0, 6.0, ((0, 16), (1, 8))),
        "out_grad": normal_values(seeds[1], (VIDEOS, F, P_SIZE, D), 1.0, 6.0, ((0, 16), (1, 8))),
        "gain_spatial": jnp.clip(1.0 + 0.18 * jax.random.normal(seeds[2], (D,), jnp.float32), 0.1, 1.9),
        "gain_temporal": jnp.clip(1.0 + 0.18 * jax.random.normal(seeds[3], (D,), jnp.float32), 0.1, 1.9),
        "w_spatial_qkv": draw_w_spatial_qkv(jax.random.fold_in(seeds[8], 71), 0),
        "w_spatial_out": normal_values(seeds[5], (D, D), D ** -0.5, 0.1875),
        "w_temporal_qkv": draw_w_temporal_qkv(jax.random.fold_in(seeds[8], 71), 0),
        "w_temporal_out": normal_values(seeds[7], (D, D), D ** -0.5, 0.1875),
    }


epsilon = 1e-06

def layer_norm(stream, gain_vec):
    center = lax.optimization_barrier(jnp.mean(stream, axis=-1, keepdims=True))
    centered = stream - center
    spread = lax.optimization_barrier(jnp.mean(centered * centered, axis=-1, keepdims=True))
    return (centered * lax.rsqrt(spread + epsilon) * gain_vec).astype(jnp.bfloat16)

def project(hidden, weight):
    return jnp.dot(hidden, weight, preferred_element_type=jnp.float32)

def split_heads(block):
    shape = block.shape[:-1] + (HEADS, block.shape[-1] // HEADS)
    return block.reshape(shape).astype(jnp.float32)

def spatial_mix(qkv):
    width = qkv.shape[-1] // 3
    query_part = split_heads(qkv[..., :width])
    key_part = split_heads(qkv[..., width:2 * width])
    value_part = split_heads(qkv[..., 2 * width:])
    scale = 1.0 / math.sqrt(width // HEADS)
    scores = jnp.einsum('bfqhd,bfkhd->bfhqk', query_part, key_part, precision=lax.Precision.HIGHEST) * scale
    weights = jax.nn.softmax(scores, axis=-1)
    mixed = jnp.einsum('bfhqk,bfkhd->bfqhd', weights, value_part, precision=lax.Precision.HIGHEST)
    return mixed.reshape(qkv.shape[:-1] + (width,)).astype(jnp.bfloat16)

def temporal_mix(qkv):
    width = qkv.shape[-1] // 3
    query_part = split_heads(qkv[..., :width])
    key_part = split_heads(qkv[..., width:2 * width])
    value_part = split_heads(qkv[..., 2 * width:])
    scale = 1.0 / math.sqrt(width // HEADS)
    scores = jnp.einsum('bqphd,bkphd->bphqk', query_part, key_part, precision=lax.Precision.HIGHEST) * scale
    weights = jax.nn.softmax(scores, axis=-1)
    mixed = jnp.einsum('bphqk,bkphd->bqphd', weights, value_part, precision=lax.Precision.HIGHEST)
    return mixed.reshape(qkv.shape[:-1] + (width,)).astype(jnp.bfloat16)

def spatial_section(clip, gain_vec, w_qkv, w_out):
    hidden = layer_norm(clip.astype(jnp.float32), gain_vec)
    qkv = project(hidden, w_qkv).astype(jnp.bfloat16)
    return clip.astype(jnp.float32) + project(spatial_mix(qkv), w_out)

def reference(video, out_grad, gain_spatial, gain_temporal, w_spatial_qkv, w_spatial_out, w_temporal_qkv, w_temporal_out):

    def one_video(carry, pair):
        clip, grad_clip = pair

        def forward(clip_in):
            stream = spatial_section(clip_in, gain_spatial, w_spatial_qkv, w_spatial_out)
            qkv = project(layer_norm(stream, gain_temporal), w_temporal_qkv).astype(jnp.bfloat16)
            mixed = temporal_mix(qkv)
            return (stream + project(mixed, w_temporal_out), mixed)
        result, back, mixed = jax.vjp(forward, clip[None], has_aux=True)
        clip_grad = back(grad_clip[None].astype(jnp.float32))[0][0]
        width = mixed.shape[-1]
        local_sum = lax.dot_general(mixed.reshape(-1, width), grad_clip.reshape(-1, width), (((0,), (0,)), ((), ())), preferred_element_type=jnp.float32)
        return (carry + local_sum, clip_grad)
    width = video.shape[-1]
    total, video_grad = lax.scan(one_video, jnp.zeros((width, width), jnp.float32), (video, out_grad))
    w_grad = total / math.sqrt(float(VIDEOS * F * P_SIZE))
    return (video_grad, w_grad)
```

```python
import math

import jax
import jax.numpy as jnp
from jax import lax
from jax.experimental import pallas as pl
from jax.experimental.pallas import tpu as pltpu
from jax.sharding import PartitionSpec as P

HEADS = 16
D = 1152
HD = D // HEADS
T = 256
SEQ = 8
POS = T // SEQ
DP = 16
EPS = 1e-06
SCALE = 1.0 / math.sqrt(HD)
BF = jnp.bfloat16
F32 = jnp.float32
ROWS = 32
WIN = 256
CHUNK = 88
OWN = D // (DP * SEQ)
LANES = 128
TILES = D // LANES

VMEM = pltpu.VMEM
ANY = pl.ANY


def nn(a, b):
    return lax.dot_general(a, b, (((1,), (0,)), ((), ())), preferred_element_type=F32)


def nt(a, b):
    return lax.dot_general(a, b, (((1,), (1,)), ((), ())), preferred_element_type=F32)


def tn(a, b):
    return lax.dot_general(a, b, (((0,), (0,)), ((), ())), preferred_element_type=F32)


def row_stats(x):
    center = jnp.mean(x, axis=-1, keepdims=True)
    centered = x - center
    spread = jnp.mean(centered * centered, axis=-1, keepdims=True)
    return centered, lax.rsqrt(spread + EPS)


def row_blocks(fn):
    def body(i, carry):
        fn(pl.ds(pl.multiple_of(i * ROWS, ROWS), ROWS))
        return carry

    lax.fori_loop(0, T // ROWS, body, 0)


def norm_back(x, g, dy):
    centered, inv = row_stats(x)
    xhat = centered * inv
    dxhat = dy * g
    mean_d = jnp.mean(dxhat, axis=-1, keepdims=True)
    mean_dx = jnp.mean(dxhat * xhat, axis=-1, keepdims=True)
    return inv * (dxhat - mean_d - xhat * mean_dx)


def window(h):
    tile = jnp.minimum(lax.div(h * HD, LANES), TILES - 2)
    low = pl.multiple_of(tile * LANES, LANES)
    start = h * HD - low
    lane = lax.broadcasted_iota(jnp.int32, (1, WIN), 1)
    inside = jnp.where((lane >= start) & (lane < start + HD), 1.0, 0.0)
    return low, inside.astype(BF)


def softmax_keys(scores):
    top = jnp.max(scores, axis=0, keepdims=True)
    e = jnp.exp((scores - top) * SCALE)
    return e * (1.0 / jnp.sum(e, axis=0, keepdims=True))


def score_grad(prob, prob_grad):
    t = prob * prob_grad
    delta = jnp.sum(t, axis=0, keepdims=True)
    return ((t - prob * delta) * SCALE).astype(BF)


def heads_loop(fn, unroll=2):
    def body(i, carry):
        for u in range(unroll):
            fn(i * unroll + u)
        return carry

    lax.fori_loop(0, HEADS // unroll, body, 0)


def fetch(src, dst, sem):
    copy = pltpu.make_async_copy(src, dst, sem)
    copy.start()
    return copy


def fetch_columns(src, dst, sems):
    out = []
    for c in range(3):
        cols = slice(c * D, (c + 1) * D)
        out.append(fetch(src.at[:, cols], dst.at[:, cols], sems.at[c]))
    return out


def spatial_forward(video, gs, gt, wq_hbm, wo_hbm, hid_out, stream_out, qkv, prob,
                    wq, wo, hid, mix, sems):
    wq_copies = fetch_columns(wq_hbm, wq, sems)
    wo_copy = fetch(wo_hbm, wo, sems.at[3])

    def first_norm(rows):
        centered, inv = row_stats(video[rows, :].astype(F32))
        hid[rows, :] = (centered * inv * gs[...]).astype(BF)

    row_blocks(first_norm)
    for c in range(3):
        cols = slice(c * D, (c + 1) * D)
        wq_copies[c].wait()
        qkv[:, cols] = nn(hid[...], wq[:, cols]).astype(BF)
    mix[...] = jnp.zeros_like(mix)

    def head(h):
        low, inside = window(h)
        q = qkv[:, pl.ds(low, WIN)] * inside
        k = qkv[:, pl.ds(D + low, WIN)]
        v = qkv[:, pl.ds(2 * D + low, WIN)] * inside
        p = softmax_keys(nt(k, q)).astype(BF)
        prob[h] = p
        mix[:, pl.ds(low, WIN)] += tn(p, v).astype(BF)

    heads_loop(head)
    wo_copy.wait()
    stream_out[...] = video[...].astype(F32) + nn(mix[...], wo[...])

    def second_norm(rows):
        centered, inv = row_stats(stream_out[rows, :])
        hid_out[rows, :] = (centered * inv * gt[...]).astype(BF)

    row_blocks(second_norm)


HALF = POS // 2
BLK = SEQ * HALF


def temporal(hid_in, dmix_in, wq_hbm, mixed_out, dhid_out,
             wq, hid, dmix, qkv, mix, dqkv, sems):
    wq_copies = fetch_columns(wq_hbm, wq, sems)
    for b in range(2):
        part = slice(b * HALF, (b + 1) * HALF)
        rows = slice(b * BLK, (b + 1) * BLK)
        hid[rows, :] = hid_in[:, part, :].reshape(BLK, D)
        dmix[rows, :] = dmix_in[:, part, :].reshape(BLK, D)
    mix[...] = jnp.zeros_like(mix)
    dqkv[...] = jnp.zeros_like(dqkv)
    for c in range(3):
        cols = slice(c * D, (c + 1) * D)
        wq_copies[c].wait()
        qkv[:, cols] = nn(hid[...], wq[:, cols]).astype(BF)

    key_pos = lax.rem(lax.broadcasted_iota(jnp.int32, (BLK, BLK), 0), HALF)
    query_pos = lax.rem(lax.broadcasted_iota(jnp.int32, (BLK, BLK), 1), HALF)
    same = key_pos == query_pos

    def head(h):
        low, inside = window(h)
        for b in range(2):
            rows = slice(b * BLK, (b + 1) * BLK)
            qs, ks, vs = pl.ds(low, WIN), pl.ds(D + low, WIN), pl.ds(2 * D + low, WIN)
            q = qkv[rows, qs] * inside
            k = qkv[rows, ks] * inside
            v = qkv[rows, vs] * inside
            do = dmix[rows, qs] * inside
            p = softmax_keys(jnp.where(same, nt(k, q), -1e30))
            pb = p.astype(BF)
            mix[rows, qs] += tn(pb, v).astype(BF)
            ds = score_grad(p, nt(v, do))
            dqkv[rows, vs] += nn(pb, do).astype(BF)
            dqkv[rows, ks] += nn(ds, q).astype(BF)
            dqkv[rows, qs] += tn(ds, k).astype(BF)

    heads_loop(head)
    dh = nt(dqkv[...], wq[...]).astype(BF)
    for b in range(2):
        part = slice(b * HALF, (b + 1) * HALF)
        rows = slice(b * BLK, (b + 1) * BLK)
        mixed_out[:, part, :] = mix[rows, :].reshape(SEQ, HALF, D)
        dhid_out[:, part, :] = dh[rows, :].reshape(SEQ, HALF, D)


def spatial_backward(dhid, stream, gt, og, qkv, prob, video, gs, wo_hbm, wq_hbm, out,
                     wo, wq, sg, sgb, dmix, dqkv, dh, sems):
    wo_copy = fetch(wo_hbm, wo, sems.at[3])
    wq_copies = fetch_columns(wq_hbm, wq, sems)

    def stream_grad(rows):
        dx = norm_back(stream[rows, :], gt[...], dhid[rows, :].astype(F32))
        total = og[rows, :].astype(F32) + dx
        sg[rows, :] = total
        sgb[rows, :] = total.astype(BF)

    row_blocks(stream_grad)
    dqkv[...] = jnp.zeros_like(dqkv)
    wo_copy.wait()
    dmix[...] = nt(sgb[...], wo[...]).astype(BF)

    def head(h):
        low, inside = window(h)
        qs, ks, vs = pl.ds(low, WIN), pl.ds(D + low, WIN), pl.ds(2 * D + low, WIN)
        q = qkv[:, qs] * inside
        k = qkv[:, ks] * inside
        v = qkv[:, vs]
        do = dmix[:, qs] * inside
        pb = prob[h]
        ds = score_grad(pb.astype(F32), nt(v, do))
        dqkv[:, vs] += nn(pb, do).astype(BF)
        dqkv[:, ks] += nn(ds, q).astype(BF)
        dqkv[:, qs] += tn(ds, k).astype(BF)

    heads_loop(head)
    for copy in wq_copies:
        copy.wait()
    dh[...] = nt(dqkv[...], wq[...]).astype(BF)

    def video_grad(rows):
        dx = norm_back(video[rows, :].astype(F32), gs[...], dh[rows, :].astype(F32))
        out[rows, :] = (sg[rows, :] + dx).astype(BF)

    row_blocks(video_grad)


GROUPS = DP // 2
PER_CORE = GROUPS * HD


def outer_product(core, mixed, og, keep, send, full):
    step = 3 * LANES
    for c in range(D // step):
        full[c * step : (c + 1) * step, :] = tn(mixed[:, c * step : (c + 1) * step], og[...])
    first = core[0] == 0
    for g in range(0, GROUPS, 2):
        even, odd = (
            jnp.concatenate(
                [full[(2 * (g + i) + c) * HD : (2 * (g + i) + c + 1) * HD, :] for i in range(2)]
            )
            for c in range(2)
        )
        rows = slice(g * HD, (g + 2) * HD)
        keep[rows, :] = jnp.where(first, even, odd)
        send[rows, :] = jnp.where(first, odd, even).astype(BF)


def add_and_cut(keep, got, out, block, cut):
    cut[...] = jnp.zeros_like(cut)

    def body(g, carry):
        rows = pl.ds(pl.multiple_of(g * HD, HD), HD)
        block[...] = keep[rows, :] + got[rows, :].astype(F32)
        for j in range(SEQ):
            for t in range(TILES):
                cut[j, t * OWN : (t + 1) * OWN, :] = block[
                    j * OWN : (j + 1) * OWN, t * LANES : (t + 1) * LANES
                ]
            out[g * SEQ + j] = cut[j].astype(BF)
        return carry

    lax.fori_loop(0, GROUPS, body, 0)


def sum_chunks(got, out, total, *, scale):
    total[...] = jnp.sum(got[...].astype(F32), axis=0) * scale
    for t in range(TILES):
        out[:, t * LANES : (t + 1) * LANES] = total[t * OWN : (t + 1) * OWN, :]


def call(fn, outs, args, scratch, flops, name, specs=None):
    if specs is None:
        specs = [VMEM] * len(args)
    moved = sum(a.size * a.dtype.itemsize for a in args)
    moved += sum(math.prod(s) * jnp.dtype(d).itemsize for s, d in outs)
    return pl.pallas_call(
        fn,
        out_shape=[jax.ShapeDtypeStruct(s, d) for s, d in outs],
        in_specs=[pl.BlockSpec(memory_space=s) for s in specs],
        out_specs=[pl.BlockSpec(memory_space=VMEM)] * len(outs),
        scratch_shapes=scratch,
        cost_estimate=pl.CostEstimate(flops=flops, bytes_accessed=moved, transcendentals=0),
        name=name,
    )(*args)


def per_device(
    video,
    out_grad,
    gain_spatial,
    gain_temporal,
    w_spatial_qkv,
    w_spatial_out,
    w_temporal_qkv,
    w_temporal_out,
):
    videos = lax.axis_size("dp") * video.shape[0]
    tokens = videos * SEQ * T
    shape = video.shape
    clip = video.reshape(T, D)
    og = out_grad.reshape(T, D)
    gs = gain_spatial.reshape(1, D)
    gt = gain_temporal.reshape(1, D)
    dma = pltpu.SemaphoreType.DMA((4,))
    wide, square = VMEM((D, 3 * D), BF), VMEM((D, D), BF)
    tok, tok3 = VMEM((T, D), BF), VMEM((T, 3 * D), BF)
    unit = 2 * T * D * D

    def exchange(x):
        return lax.all_to_all(x.reshape(SEQ, POS, D), "seq", 0, 0, tiled=True)

    og_pos = exchange(og)
    hid, stream, qkv, prob = call(
        spatial_forward,
        [((T, D), BF), ((T, D), F32), ((T, 3 * D), BF), ((HEADS, T, T), BF)],
        (clip, gs, gt, w_spatial_qkv, w_spatial_out),
        [wide, square, tok, tok, dma],
        5 * unit,
        "spatial_forward",
        [VMEM, VMEM, VMEM, ANY, ANY],
    )
    hid_pos = exchange(hid)
    dmix = nt(og_pos.reshape(T, D), w_temporal_out).astype(BF).reshape(SEQ, POS, D)
    mixed_pos, dhid_pos = call(
        temporal,
        [((SEQ, POS, D), BF), ((SEQ, POS, D), BF)],
        (hid_pos, dmix, w_temporal_qkv),
        [wide, tok, tok, tok3, tok, tok3, dma],
        8 * unit,
        "temporal",
        [VMEM, VMEM, ANY],
    )
    dhid = exchange(dhid_pos).reshape(T, D)

    core = lax.rem(lax.axis_index("dp"), 2).reshape(1)
    keep, send = call(
        outer_product,
        [((PER_CORE, D), F32), ((PER_CORE, D), BF)],
        (core, mixed_pos.reshape(T, D), og_pos.reshape(T, D)),
        [VMEM((D, D), F32)],
        unit,
        "outer_product",
        [pltpu.SMEM, VMEM, VMEM],
    )
    got = lax.ppermute(send, "dp", [(i, i ^ 1) for i in range(DP)])
    chunks = call(
        add_and_cut,
        [((GROUPS * SEQ, CHUNK, LANES), BF)],
        (keep, got),
        [VMEM((HD, D), F32), VMEM((SEQ, CHUNK, LANES), F32)],
        unit,
        "add_and_cut",
    )[0]
    chunks, dhid = lax.optimization_barrier((chunks, dhid))
    owners = [
        [(g * 2 + c) * SEQ + s for g in range(GROUPS) for s in range(SEQ)] for c in range(2)
    ]
    parts = lax.all_to_all(
        chunks, ("dp", "seq"), 0, 0, axis_index_groups=owners, tiled=True
    )
    video_grad = call(
        spatial_backward,
        [((T, D), BF)],
        (dhid, stream, gt, og, qkv, prob, clip, gs, w_spatial_out, w_spatial_qkv),
        [square, wide, VMEM((T, D), F32), tok, tok, tok3, tok, dma],
        7 * unit,
        "spatial_backward",
        [VMEM] * 8 + [ANY] * 2,
    )[0]

    def finish(got_ref, out_ref, total_ref):
        sum_chunks(got_ref, out_ref, total_ref, scale=1.0 / math.sqrt(float(tokens)))

    w_grad = call(
        finish,
        [((OWN, D), F32)],
        (parts,),
        [VMEM((CHUNK, LANES), F32)],
        1000,
        "sum_chunks",
    )[0]
    return (video_grad.reshape(shape), w_grad)


def solution(mesh):
    return jax.shard_map(
        per_device,
        mesh=mesh,
        in_specs=(
            P("dp", "seq", None, None),
            P("dp", "seq", None, None),
            P(),
            P(),
            P(),
            P(),
            P(),
            P(),
        ),
        out_specs=(P("dp", "seq", None, None), P(("dp", "seq"), None)),
        check_vma=False,
    )
```

```python
import math

import jax
import jax.numpy as jnp
from jax import lax
from jax.experimental import pallas as pl
from jax.experimental.pallas import tpu as pltpu
from jax.sharding import PartitionSpec as P


HEADS = 16
D = 1152
HD = D // HEADS
T = 256
SEQ = 8
POS = T // SEQ
DP = 16
EPS = 1e-06
LOG2E = 1.0 / math.log(2.0)
SCALE = 1.0 / math.sqrt(HD)
BF = jnp.bfloat16
F32 = jnp.float32
ROWS = 32
WIN = 256
CHUNK = 88
OWN = D // (DP * SEQ)
LANES = 128
TILES = D // LANES

VMEM = pltpu.VMEM
ANY = pl.ANY


def nn(a, b):
    return lax.dot_general(a, b, (((1,), (0,)), ((), ())), preferred_element_type=F32)


def nt(a, b):
    return lax.dot_general(a, b, (((1,), (1,)), ((), ())), preferred_element_type=F32)


def tn(a, b):
    return lax.dot_general(a, b, (((0,), (0,)), ((), ())), preferred_element_type=F32)


def row_stats(x):
    center = jnp.mean(x, axis=-1, keepdims=True)
    centered = x - center
    spread = jnp.mean(centered * centered, axis=-1, keepdims=True)
    return centered, lax.rsqrt(spread + EPS)


def row_blocks(fn):
    def body(i, carry):
        fn(pl.ds(pl.multiple_of(i * ROWS, ROWS), ROWS))
        return carry

    lax.fori_loop(0, T // ROWS, body, 0)


def norm_back(x, g, dy):
    centered, inv = row_stats(x)
    xhat = centered * inv
    dxhat = dy * g
    mean_d = jnp.mean(dxhat, axis=-1, keepdims=True)
    mean_dx = jnp.mean(dxhat * xhat, axis=-1, keepdims=True)
    return inv * (dxhat - mean_d - xhat * mean_dx)


def window(h):
    tile = jnp.minimum(lax.div(h * HD, LANES), TILES - 2)
    low = pl.multiple_of(tile * LANES, LANES)
    start = h * HD - low
    lane = lax.broadcasted_iota(jnp.int32, (1, WIN), 1)
    inside = jnp.where((lane >= start) & (lane < start + HD), 1.0, 0.0)
    return low, inside.astype(BF)


def softmax_keys(scores):
    top = jnp.max(scores, axis=0, keepdims=True)
    e = jnp.exp2((scores - top) * (SCALE * LOG2E))
    return e * (1.0 / jnp.sum(e, axis=0, keepdims=True))


def score_grad(prob, prob_grad):
    t = prob * prob_grad
    delta = jnp.sum(t, axis=0, keepdims=True)
    return ((t - prob * delta) * SCALE).astype(BF)


def heads_loop(first, second, unroll=8, ahead=1):
    def body(i, carry):
        waiting = []
        for u in range(unroll):
            h = i * unroll + u
            waiting.append((h, first(h)))
            if len(waiting) > ahead:
                h, values = waiting.pop(0)
                second(h, *values)
        for h, values in waiting:
            second(h, *values)
        return carry

    lax.fori_loop(0, HEADS // unroll, body, 0)


def merge(slots, dst, base=0):
    for t in range(TILES):
        total = None
        for h in range(HEADS):
            first = min(h * HD // LANES, TILES - 2)
            if h * HD < (t + 1) * LANES and (h + 1) * HD > t * LANES:
                at = (t - first) * LANES
                piece = slots[h, :, at : at + LANES]
                total = piece if total is None else total + piece
        dst[:, base + t * LANES : base + (t + 1) * LANES] = total


def fetch(src, dst, sem):
    copy = pltpu.make_async_copy(src, dst, sem)
    copy.start()
    return copy


CUTS = (0, 512, 1536, 2560, 3456)
PIECES = [slice(a, b) for a, b in zip(CUTS, CUTS[1:])]


def fetch_columns(src, dst, sems):
    return [fetch(src.at[:, p], dst.at[:, p], sems.at[i]) for i, p in enumerate(PIECES)]


def spatial_forward(video, gs, gt, wq_hbm, wo_hbm, hid_out, stream_hbm, qkv_hbm, prob_hbm,
                    wq, wo, hid, mix, stream, qkv, prob, slots, sems, out_sems):
    wq_copies = fetch_columns(wq_hbm, wq, sems)
    wo_copy = fetch(wo_hbm, wo, sems.at[4])

    def first_norm(rows):
        centered, inv = row_stats(video[rows, :].astype(F32))
        hid[rows, :] = (centered * inv * gs[...].reshape(1, D)).astype(BF)

    row_blocks(first_norm)
    for copy, p in zip(wq_copies, PIECES):
        copy.wait()
        qkv[:, p] = nn(hid[...], wq[:, p]).astype(BF)
    qkv_copy = fetch(qkv, qkv_hbm, out_sems.at[0])

    def head(h):
        low, inside = window(h)
        q = qkv[:, pl.ds(low, WIN)] * inside
        k = qkv[:, pl.ds(D + low, WIN)]
        v = qkv[:, pl.ds(2 * D + low, WIN)] * inside
        return nt(k, q), v

    def rest(h, scores, v):
        p = softmax_keys(scores).astype(BF)
        prob[h] = p
        slots[h] = tn(p, v).astype(BF)

    heads_loop(head, rest)
    prob_copy = fetch(prob, prob_hbm, out_sems.at[1])
    merge(slots, mix)
    wo_copy.wait()
    stream[...] = video[...].astype(F32) + nn(mix[...], wo[...])
    stream_copy = fetch(stream, stream_hbm, out_sems.at[2])

    def second_norm(rows):
        centered, inv = row_stats(stream[rows, :])
        hid_out[rows, :] = (centered * inv * gt[...].reshape(1, D)).astype(BF)

    row_blocks(second_norm)
    for copy in (qkv_copy, prob_copy, stream_copy):
        copy.wait()


HALF = POS // 2
BLK = SEQ * HALF


def temporal(hid_in, dmix_in, wq_hbm, mixed_out, dhid_out,
             wq, hid, dmix, qkv, mix, dqkv, o_slots, q_slots, k_slots, v_slots, sems):
    wq_copies = fetch_columns(wq_hbm, wq, sems)
    for b in range(2):
        part = slice(b * HALF, (b + 1) * HALF)
        rows = slice(b * BLK, (b + 1) * BLK)
        hid[rows, :] = hid_in[:, part, :].reshape(BLK, D)
        dmix[rows, :] = dmix_in[:, part, :].reshape(BLK, D)
    for copy, p in zip(wq_copies, PIECES):
        copy.wait()
        qkv[:, p] = nn(hid[...], wq[:, p]).astype(BF)

    key_pos = lax.rem(lax.broadcasted_iota(jnp.int32, (BLK, BLK), 0), HALF)
    query_pos = lax.rem(lax.broadcasted_iota(jnp.int32, (BLK, BLK), 1), HALF)
    same = key_pos == query_pos

    def head(h):
        low, inside = window(h)
        values = []
        for b in range(2):
            rows = slice(b * BLK, (b + 1) * BLK)
            qs, ks, vs = pl.ds(low, WIN), pl.ds(D + low, WIN), pl.ds(2 * D + low, WIN)
            q = qkv[rows, qs] * inside
            k = qkv[rows, ks] * inside
            v = qkv[rows, vs] * inside
            do = dmix[rows, qs] * inside
            values.append((nt(k, q), nt(v, do), q, k, v, do))
        return values

    def rest(h, *values):
        for b, (scores, prob_grad, q, k, v, do) in enumerate(values):
            rows = slice(b * BLK, (b + 1) * BLK)
            p = softmax_keys(jnp.where(same, scores, -1e30))
            pb = p.astype(BF)
            ds = score_grad(p, prob_grad)
            o_slots[h, rows, :] = tn(pb, v).astype(BF)
            v_slots[h, rows, :] = nn(pb, do).astype(BF)
            k_slots[h, rows, :] = nn(ds, q).astype(BF)
            q_slots[h, rows, :] = tn(ds, k).astype(BF)

    heads_loop(head, rest)
    merge(o_slots, mix)
    for i, slots in enumerate((q_slots, k_slots, v_slots)):
        merge(slots, dqkv, i * D)
    dh = nt(dqkv[...], wq[...]).astype(BF)
    for b in range(2):
        part = slice(b * HALF, (b + 1) * HALF)
        rows = slice(b * BLK, (b + 1) * BLK)
        mixed_out[:, part, :] = mix[rows, :].reshape(SEQ, HALF, D)
        dhid_out[:, part, :] = dh[rows, :].reshape(SEQ, HALF, D)


def spatial_backward(dhid_hbm, stream_hbm, gt, og_hbm, qkv_hbm, prob_hbm, video_hbm, gs,
                     wo_hbm, wq_hbm, out, dhid, stream, og, qkv, prob, video, wo, wq,
                     sg, sgb, dmix, dqkv, dh, q_slots, k_slots, v_slots, sems):
    pairs = (
        (dhid_hbm, dhid), (stream_hbm, stream), (og_hbm, og), (wo_hbm, wo), (qkv_hbm, qkv),
        (prob_hbm, prob), (wq_hbm, wq), (video_hbm, video),
    )
    copies = [fetch(src, dst, sems.at[i]) for i, (src, dst) in enumerate(pairs)]
    for copy in copies[:3]:
        copy.wait()

    def stream_grad(rows):
        dx = norm_back(stream[rows, :], gt[...].reshape(1, D), dhid[rows, :].astype(F32))
        total = og[rows, :].astype(F32) + dx
        sg[rows, :] = total
        sgb[rows, :] = total.astype(BF)

    row_blocks(stream_grad)
    copies[3].wait()
    dmix[...] = nt(sgb[...], wo[...]).astype(BF)
    copies[4].wait()
    copies[5].wait()

    def head(h):
        low, inside = window(h)
        qs, ks, vs = pl.ds(low, WIN), pl.ds(D + low, WIN), pl.ds(2 * D + low, WIN)
        q = qkv[:, qs] * inside
        k = qkv[:, ks] * inside
        v = qkv[:, vs]
        do = dmix[:, qs] * inside
        return nt(v, do), q, k, do

    def rest(h, prob_grad, q, k, do):
        pb = prob[h]
        ds = score_grad(pb.astype(F32), prob_grad)
        v_slots[h] = nn(pb, do).astype(BF)
        k_slots[h] = nn(ds, q).astype(BF)
        q_slots[h] = tn(ds, k).astype(BF)

    heads_loop(head, rest)
    for i, slots in enumerate((q_slots, k_slots, v_slots)):
        merge(slots, dqkv, i * D)
    copies[6].wait()
    dh[...] = nt(dqkv[...], wq[...]).astype(BF)
    copies[7].wait()

    def video_grad(rows):
        dx = norm_back(video[rows, :].astype(F32), gs[...].reshape(1, D), dh[rows, :].astype(F32))
        out[rows, :] = (sg[rows, :] + dx).astype(BF)

    row_blocks(video_grad)


GROUPS = DP // 2
PER_CORE = GROUPS * HD


def outer_product(core, mixed, og, keep, send, full):
    step = 3 * LANES
    for c in range(D // step):
        full[c * step : (c + 1) * step, :] = tn(mixed[:, c * step : (c + 1) * step], og[...])
    first = core[0] == 0
    for g in range(0, GROUPS, 2):
        even, odd = (
            jnp.concatenate(
                [full[(2 * (g + i) + c) * HD : (2 * (g + i) + c + 1) * HD, :] for i in range(2)]
            )
            for c in range(2)
        )
        rows = slice(g * HD, (g + 2) * HD)
        keep[rows, :] = jnp.where(first, even, odd).astype(BF)
        send[rows, :] = jnp.where(first, odd, even).astype(BF)


SUB = 8


def add_and_cut(keep, got, out, block):
    place = lax.broadcasted_iota(jnp.int32, (SUB, 1), 0)

    def body(g, carry):
        rows = pl.ds(pl.multiple_of(g * 2 * HD, 2 * HD), 2 * HD)
        block[...] = keep[rows, :].astype(F32) + got[rows, :].astype(F32)
        for i in range(2):
            for j in range(SEQ):
                at = i * HD + j * SUB
                upper, lower = block[at : at + SUB, :], block[at + SUB : at + 2 * SUB, :]
                eight = jnp.where(place >= j, upper, lower)
                ninth = lower[j : j + 1, :]
                parts = [eight[:, t * LANES : (t + 1) * LANES] for t in range(TILES)]
                for first in (0, SUB):
                    rest = jnp.zeros((SUB, LANES), F32)
                    for t in range(first, min(first + SUB, TILES)):
                        rest = jnp.where(
                            place == t - first, ninth[:, t * LANES : (t + 1) * LANES], rest
                        )
                    parts.append(rest)
                out[(g * 2 + i) * SEQ + j] = jnp.concatenate(parts).astype(BF)
        return carry

    lax.fori_loop(0, GROUPS // 2, body, 0)


def sum_chunks(owner, got, out, total, *, scale):
    total[...] = jnp.sum(got[...].astype(F32), axis=0) * scale
    back = lax.rem(SUB - owner[0], SUB)
    for t in range(TILES):
        lanes = slice(t * LANES, (t + 1) * LANES)
        out[:SUB, lanes] = pltpu.roll(total[t * SUB : (t + 1) * SUB, :], back, 0)
        out[SUB:, lanes] = total[TILES * SUB + t : TILES * SUB + t + 1, :]


def call(fn, outs, args, scratch, flops, specs=None, out_specs=None):
    if specs is None:
        specs = [VMEM] * len(args)
    if out_specs is None:
        out_specs = [VMEM] * len(outs)
    moved = sum(a.size * a.dtype.itemsize for a in args)
    moved += sum(math.prod(s) * jnp.dtype(d).itemsize for s, d in outs)
    return pl.pallas_call(
        fn,
        out_shape=[jax.ShapeDtypeStruct(s, d) for s, d in outs],
        in_specs=[pl.BlockSpec(memory_space=s) for s in specs],
        out_specs=[pl.BlockSpec(memory_space=s) for s in out_specs],
        scratch_shapes=scratch,
        cost_estimate=pl.CostEstimate(flops=flops, bytes_accessed=moved, transcendentals=0),
    )(*args)


UNIT = 2 * T * D * D
WIDE, SQUARE = VMEM((D, 3 * D), BF), VMEM((D, D), BF)
TOK, TOK3, TOKF = VMEM((T, D), BF), VMEM((T, 3 * D), BF), VMEM((T, D), F32)
PROB, SLOTS = VMEM((HEADS, T, T), BF), VMEM((HEADS, T, WIN), BF)
DMA = pltpu.SemaphoreType.DMA


def run_spatial_forward(clip, gs, gt, wq, wo):
    return call(
        spatial_forward,
        [((T, D), BF), ((T, D), F32), ((T, 3 * D), BF), ((HEADS, T, T), BF)],
        (clip, gs, gt, wq, wo),
        [WIDE, SQUARE, TOK, TOK, TOKF, TOK3, PROB, SLOTS, DMA((5,)), DMA((3,))],
        5 * UNIT,
        [VMEM, VMEM, VMEM, ANY, ANY],
        [VMEM, ANY, ANY, ANY],
    )


def run_temporal(hid, dmix, wq):
    return call(
        temporal,
        [((SEQ, POS, D), BF), ((SEQ, POS, D), BF)],
        (hid, dmix, wq),
        [WIDE, TOK, TOK, TOK3, TOK, TOK3, SLOTS, SLOTS, SLOTS, SLOTS, DMA((4,))],
        8 * UNIT,
        [VMEM, VMEM, ANY],
    )


def run_spatial_backward(dhid, stream, gt, og, qkv, prob, clip, gs, wo, wq):
    return call(
        spatial_backward,
        [((T, D), BF)],
        (dhid, stream, gt, og, qkv, prob, clip, gs, wo, wq),
        [TOK, TOKF, TOK, TOK3, PROB, TOK, SQUARE, WIDE, TOKF, TOK, TOK, TOK3, TOK,
         SLOTS, SLOTS, SLOTS, DMA((8,))],
        7 * UNIT,
        [ANY, ANY, VMEM, ANY, ANY, ANY, ANY, VMEM, ANY, ANY],
    )[0]


def run_outer_product(core, mixed, og):
    return call(
        outer_product,
        [((PER_CORE, D), BF), ((PER_CORE, D), BF)],
        (core, mixed, og),
        [VMEM((D, D), F32)],
        UNIT,
        [pltpu.SMEM, VMEM, VMEM],
    )


def run_add_and_cut(keep, got):
    return call(
        add_and_cut,
        [((GROUPS * SEQ, CHUNK, LANES), BF)],
        (keep, got),
        [VMEM((2 * HD, D), F32)],
        UNIT // 4,
    )[0]


def run_sum_chunks(owner, parts, scale):
    def finish(owner_ref, got_ref, out_ref, total_ref):
        sum_chunks(owner_ref, got_ref, out_ref, total_ref, scale=scale)

    return call(
        finish,
        [((OWN, D), F32)],
        (owner, parts),
        [VMEM((CHUNK, LANES), F32)],
        1000,
        [pltpu.SMEM, VMEM],
    )[0]


def per_device(
    video,
    out_grad,
    gain_spatial,
    gain_temporal,
    w_spatial_qkv,
    w_spatial_out,
    w_temporal_qkv,
    w_temporal_out,
):
    tokens = lax.axis_size("dp") * video.shape[0] * SEQ * T
    shape = video.shape
    clip = video.reshape(T, D)
    og = out_grad.reshape(T, D)

    def exchange(x):
        return lax.all_to_all(x.reshape(SEQ, POS, D), "seq", 0, 0, tiled=True)

    og_pos = exchange(og)
    hid, stream, qkv, prob = run_spatial_forward(
        clip, gain_spatial, gain_temporal, w_spatial_qkv, w_spatial_out
    )
    hid_pos = exchange(hid)
    dmix = nt(og_pos.reshape(T, D), w_temporal_out).astype(BF).reshape(SEQ, POS, D)
    mixed_pos, dhid_pos = run_temporal(hid_pos, dmix, w_temporal_qkv)
    dhid = exchange(dhid_pos).reshape(T, D)

    core = lax.rem(lax.axis_index("dp"), 2).reshape(1)
    keep, send = run_outer_product(core, mixed_pos.reshape(T, D), og_pos.reshape(T, D))
    got = lax.ppermute(send, "dp", [(i, i ^ 1) for i in range(DP)])
    chunks = run_add_and_cut(keep, got)
    chunks, dhid = lax.optimization_barrier((chunks, dhid))
    owners = [
        [(g * 2 + c) * SEQ + s for g in range(GROUPS) for s in range(SEQ)] for c in range(2)
    ]
    parts = lax.all_to_all(
        chunks, ("dp", "seq"), 0, 0, axis_index_groups=owners, tiled=True
    )
    video_grad = run_spatial_backward(
        dhid, stream, gain_temporal, og, qkv, prob, clip, gain_spatial,
        w_spatial_out, w_spatial_qkv,
    )
    owner = lax.axis_index("seq").reshape(1)
    w_grad = run_sum_chunks(owner, parts, 1.0 / math.sqrt(float(tokens)))
    return (video_grad.reshape(shape), w_grad)


def solution(mesh):
    return jax.shard_map(
        per_device,
        mesh=mesh,
        in_specs=(
            P("dp", "seq", None, None),
            P("dp", "seq", None, None),
            P(),
            P(),
            P(),
            P(),
            P(),
            P(),
        ),
        out_specs=(P("dp", "seq", None, None), P(("dp", "seq"), None)),
        check_vma=False,
    )
```

```python
import math

import jax
import jax.numpy as jnp
from jax import lax
from jax.experimental import pallas as pl
from jax.experimental.pallas import tpu as pltpu
from jax.sharding import PartitionSpec as P


HEADS = 16
D = 1152
HD = D // HEADS
T = 256
SEQ = 8
POS = T // SEQ
DP = 16
EPS = 1e-06
LOG2E = 1.0 / math.log(2.0)
SCALE = 1.0 / math.sqrt(HD)
BF = jnp.bfloat16
F32 = jnp.float32
ROWS = 32
WIN = 256
CHUNK = 88
OWN = D // (DP * SEQ)
LANES = 128
TILES = D // LANES

VMEM = pltpu.VMEM
ANY = pl.ANY


def nn(a, b):
    return lax.dot_general(a, b, (((1,), (0,)), ((), ())), preferred_element_type=F32)


def nt(a, b):
    return lax.dot_general(a, b, (((1,), (1,)), ((), ())), preferred_element_type=F32)


def tn(a, b):
    return lax.dot_general(a, b, (((0,), (0,)), ((), ())), preferred_element_type=F32)


def row_stats(x):
    center = jnp.mean(x, axis=-1, keepdims=True)
    centered = x - center
    spread = jnp.mean(centered * centered, axis=-1, keepdims=True)
    return centered, lax.rsqrt(spread + EPS)


def row_blocks(fn):
    def body(i, carry):
        fn(pl.ds(pl.multiple_of(i * ROWS, ROWS), ROWS))
        return carry

    lax.fori_loop(0, T // ROWS, body, 0)


def norm_back(x, g, dy):
    centered, inv = row_stats(x)
    xhat = centered * inv
    dxhat = dy * g
    mean_d = jnp.mean(dxhat, axis=-1, keepdims=True)
    mean_dx = jnp.mean(dxhat * xhat, axis=-1, keepdims=True)
    return inv * (dxhat - mean_d - xhat * mean_dx)


def window(h):
    tile = jnp.minimum(lax.div(h * HD, LANES), TILES - 2)
    low = pl.multiple_of(tile * LANES, LANES)
    start = h * HD - low
    lane = lax.broadcasted_iota(jnp.int32, (1, WIN), 1)
    inside = jnp.where((lane >= start) & (lane < start + HD), 1.0, 0.0)
    return low, inside.astype(BF)


def softmax_keys(scores):
    top = jnp.max(scores, axis=0, keepdims=True)
    e = jnp.exp2((scores - top) * (SCALE * LOG2E))
    return e * (1.0 / jnp.sum(e, axis=0, keepdims=True))


def score_grad(prob, prob_grad):
    t = prob * prob_grad
    delta = jnp.sum(t, axis=0, keepdims=True)
    return ((t - prob * delta) * SCALE).astype(BF)


def heads_loop(first, second, unroll=8, ahead=1):
    def body(i, carry):
        waiting = []
        for u in range(unroll):
            h = i * unroll + u
            waiting.append((h, first(h)))
            if len(waiting) > ahead:
                h, values = waiting.pop(0)
                second(h, *values)
        for h, values in waiting:
            second(h, *values)
        return carry

    lax.fori_loop(0, HEADS // unroll, body, 0)


def merge(slots, dst, base=0):
    for t in range(TILES):
        total = None
        for h in range(HEADS):
            first = min(h * HD // LANES, TILES - 2)
            if h * HD < (t + 1) * LANES and (h + 1) * HD > t * LANES:
                at = (t - first) * LANES
                piece = slots[h, :, at : at + LANES]
                total = piece if total is None else total + piece
        dst[:, base + t * LANES : base + (t + 1) * LANES] = total


def fetch(src, dst, sem):
    copy = pltpu.make_async_copy(src, dst, sem)
    copy.start()
    return copy


CUTS = (0, 512, 1536, 2560, 3456)
PIECES = [slice(a, b) for a, b in zip(CUTS, CUTS[1:])]


def fetch_columns(src, dst, sems):
    return [fetch(src.at[:, p], dst.at[:, p], sems.at[i]) for i, p in enumerate(PIECES)]


def spatial_forward(video, gs, gt, wq_hbm, wo_hbm, hid_out, stream_hbm, qkv_hbm, prob_hbm,
                    wq, wo, hid, mix, stream, qkv, prob, slots, sems, out_sems):
    wq_copies = fetch_columns(wq_hbm, wq, sems)
    wo_copy = fetch(wo_hbm, wo, sems.at[4])

    def first_norm(rows):
        centered, inv = row_stats(video[rows, :].astype(F32))
        hid[rows, :] = (centered * inv * gs[...].reshape(1, D)).astype(BF)

    row_blocks(first_norm)
    for copy, p in zip(wq_copies, PIECES):
        copy.wait()
        qkv[:, p] = nn(hid[...], wq[:, p]).astype(BF)
    qkv_copy = fetch(qkv, qkv_hbm, out_sems.at[0])

    def head(h):
        low, inside = window(h)
        q = qkv[:, pl.ds(low, WIN)] * inside
        k = qkv[:, pl.ds(D + low, WIN)]
        v = qkv[:, pl.ds(2 * D + low, WIN)] * inside
        return nt(k, q), v

    def rest(h, scores, v):
        p = softmax_keys(scores).astype(BF)
        prob[h] = p
        slots[h] = tn(p, v).astype(BF)

    heads_loop(head, rest)
    prob_copy = fetch(prob, prob_hbm, out_sems.at[1])
    merge(slots, mix)
    wo_copy.wait()
    stream[...] = video[...].astype(F32) + nn(mix[...], wo[...])
    stream_copy = fetch(stream, stream_hbm, out_sems.at[2])

    def second_norm(rows):
        centered, inv = row_stats(stream[rows, :])
        hid_out[rows, :] = (centered * inv * gt[...].reshape(1, D)).astype(BF)

    row_blocks(second_norm)
    for copy in (qkv_copy, prob_copy, stream_copy):
        copy.wait()


HALF = POS // 2
BLK = SEQ * HALF


def temporal(hid_in, dmix_in, wq_hbm, mixed_out, dhid_out,
             wq, hid, dmix, qkv, mix, dqkv, o_slots, q_slots, k_slots, v_slots, sems):
    wq_copies = fetch_columns(wq_hbm, wq, sems)
    for b in range(2):
        part = slice(b * HALF, (b + 1) * HALF)
        rows = slice(b * BLK, (b + 1) * BLK)
        hid[rows, :] = hid_in[:, part, :].reshape(BLK, D)
        dmix[rows, :] = dmix_in[:, part, :].reshape(BLK, D)
    for copy, p in zip(wq_copies, PIECES):
        copy.wait()
        qkv[:, p] = nn(hid[...], wq[:, p]).astype(BF)

    key_pos = lax.rem(lax.broadcasted_iota(jnp.int32, (BLK, BLK), 0), HALF)
    query_pos = lax.rem(lax.broadcasted_iota(jnp.int32, (BLK, BLK), 1), HALF)
    same = key_pos == query_pos

    def head(h):
        low, inside = window(h)
        values = []
        for b in range(2):
            rows = slice(b * BLK, (b + 1) * BLK)
            qs, ks, vs = pl.ds(low, WIN), pl.ds(D + low, WIN), pl.ds(2 * D + low, WIN)
            q = qkv[rows, qs] * inside
            k = qkv[rows, ks] * inside
            v = qkv[rows, vs] * inside
            do = dmix[rows, qs] * inside
            values.append((nt(k, q), nt(v, do), q, k, v, do))
        return values

    def rest(h, *values):
        for b, (scores, prob_grad, q, k, v, do) in enumerate(values):
            rows = slice(b * BLK, (b + 1) * BLK)
            p = softmax_keys(jnp.where(same, scores, -1e30))
            pb = p.astype(BF)
            ds = score_grad(p, prob_grad)
            o_slots[h, rows, :] = tn(pb, v).astype(BF)
            v_slots[h, rows, :] = nn(pb, do).astype(BF)
            k_slots[h, rows, :] = nn(ds, q).astype(BF)
            q_slots[h, rows, :] = tn(ds, k).astype(BF)

    heads_loop(head, rest)
    merge(o_slots, mix)
    for i, slots in enumerate((q_slots, k_slots, v_slots)):
        merge(slots, dqkv, i * D)
    dh = nt(dqkv[...], wq[...]).astype(BF)
    for b in range(2):
        part = slice(b * HALF, (b + 1) * HALF)
        rows = slice(b * BLK, (b + 1) * BLK)
        mixed_out[:, part, :] = mix[rows, :].reshape(SEQ, HALF, D)
        dhid_out[:, part, :] = dh[rows, :].reshape(SEQ, HALF, D)


def spatial_backward(dhid_hbm, stream_hbm, gt, og_hbm, qkv_hbm, prob_hbm, video_hbm, gs,
                     wo_hbm, wq_hbm, out, dhid, stream, og, qkv, prob, video, wo, wq,
                     sg, sgb, dmix, dqkv, dh, q_slots, k_slots, v_slots, sems):
    pairs = (
        (dhid_hbm, dhid), (stream_hbm, stream), (og_hbm, og), (wo_hbm, wo), (qkv_hbm, qkv),
        (prob_hbm, prob), (wq_hbm, wq), (video_hbm, video),
    )
    copies = [fetch(src, dst, sems.at[i]) for i, (src, dst) in enumerate(pairs)]
    for copy in copies[:3]:
        copy.wait()

    def stream_grad(rows):
        dx = norm_back(stream[rows, :], gt[...].reshape(1, D), dhid[rows, :].astype(F32))
        total = og[rows, :].astype(F32) + dx
        sg[rows, :] = total
        sgb[rows, :] = total.astype(BF)

    row_blocks(stream_grad)
    copies[3].wait()
    dmix[...] = nt(sgb[...], wo[...]).astype(BF)
    copies[4].wait()
    copies[5].wait()

    def head(h):
        low, inside = window(h)
        qs, ks, vs = pl.ds(low, WIN), pl.ds(D + low, WIN), pl.ds(2 * D + low, WIN)
        q = qkv[:, qs] * inside
        k = qkv[:, ks] * inside
        v = qkv[:, vs]
        do = dmix[:, qs] * inside
        return nt(v, do), q, k, do

    def rest(h, prob_grad, q, k, do):
        pb = prob[h]
        ds = score_grad(pb.astype(F32), prob_grad)
        v_slots[h] = nn(pb, do).astype(BF)
        k_slots[h] = nn(ds, q).astype(BF)
        q_slots[h] = tn(ds, k).astype(BF)

    heads_loop(head, rest)
    for i, slots in enumerate((q_slots, k_slots, v_slots)):
        merge(slots, dqkv, i * D)
    copies[6].wait()
    dh[...] = nt(dqkv[...], wq[...]).astype(BF)
    copies[7].wait()

    def video_grad(rows):
        dx = norm_back(video[rows, :].astype(F32), gs[...].reshape(1, D), dh[rows, :].astype(F32))
        out[rows, :] = (sg[rows, :] + dx).astype(BF)

    row_blocks(video_grad)


GROUPS = DP // 2


SUB = 8


def outer_product(core, mixed, other_mixed, og, other_og, out, m, g, full, sems):
    copies = [
        fetch(mixed, m.at[:T, :], sems.at[0]),
        fetch(og, g.at[:T, :], sems.at[1]),
        fetch(other_mixed, m.at[T:, :], sems.at[2]),
        fetch(other_og, g.at[T:, :], sems.at[3]),
    ]
    for copy in copies:
        copy.wait()
    step = 3 * LANES
    for c in range(D // step):
        full[c * step : (c + 1) * step, :] = tn(m[:, c * step : (c + 1) * step], g[...])
    place = lax.broadcasted_iota(jnp.int32, (SUB, 1), 0)

    def body(i, carry):
        base = (2 * i + core[0]) * HD
        for j in range(SEQ):
            at = base + j * SUB
            upper = full[pl.ds(pl.multiple_of(at, SUB), SUB), :]
            lower = full[pl.ds(pl.multiple_of(at + SUB, SUB), SUB), :]
            eight = jnp.where(place >= j, upper, lower)
            ninth = lower[j : j + 1, :]
            parts = [eight[:, t * LANES : (t + 1) * LANES] for t in range(TILES)]
            for first in (0, SUB):
                rest = jnp.zeros((SUB, LANES), F32)
                for t in range(first, min(first + SUB, TILES)):
                    rest = jnp.where(
                        place == t - first, ninth[:, t * LANES : (t + 1) * LANES], rest
                    )
                parts.append(rest)
            out[i * SEQ + j] = jnp.concatenate(parts).astype(BF)
        return carry

    lax.fori_loop(0, GROUPS, body, 0)


def sum_chunks(owner, got, out, total, *, scale):
    total[...] = jnp.sum(got[...].astype(F32), axis=0) * scale
    back = lax.rem(SUB - owner[0], SUB)
    for t in range(TILES):
        lanes = slice(t * LANES, (t + 1) * LANES)
        out[:SUB, lanes] = pltpu.roll(total[t * SUB : (t + 1) * SUB, :], back, 0)
        out[SUB:, lanes] = total[TILES * SUB + t : TILES * SUB + t + 1, :]


def call(fn, outs, args, scratch, flops, specs=None, out_specs=None):
    if specs is None:
        specs = [VMEM] * len(args)
    if out_specs is None:
        out_specs = [VMEM] * len(outs)
    moved = sum(a.size * a.dtype.itemsize for a in args)
    moved += sum(math.prod(s) * jnp.dtype(d).itemsize for s, d in outs)
    return pl.pallas_call(
        fn,
        out_shape=[jax.ShapeDtypeStruct(s, d) for s, d in outs],
        in_specs=[pl.BlockSpec(memory_space=s) for s in specs],
        out_specs=[pl.BlockSpec(memory_space=s) for s in out_specs],
        scratch_shapes=scratch,
        cost_estimate=pl.CostEstimate(flops=flops, bytes_accessed=moved, transcendentals=0),
    )(*args)


UNIT = 2 * T * D * D
WIDE, SQUARE = VMEM((D, 3 * D), BF), VMEM((D, D), BF)
TOK, TOK3, TOKF = VMEM((T, D), BF), VMEM((T, 3 * D), BF), VMEM((T, D), F32)
PROB, SLOTS = VMEM((HEADS, T, T), BF), VMEM((HEADS, T, WIN), BF)
DMA = pltpu.SemaphoreType.DMA


def run_spatial_forward(clip, gs, gt, wq, wo):
    return call(
        spatial_forward,
        [((T, D), BF), ((T, D), F32), ((T, 3 * D), BF), ((HEADS, T, T), BF)],
        (clip, gs, gt, wq, wo),
        [WIDE, SQUARE, TOK, TOK, TOKF, TOK3, PROB, SLOTS, DMA((5,)), DMA((3,))],
        5 * UNIT,
        [VMEM, VMEM, VMEM, ANY, ANY],
        [VMEM, ANY, ANY, ANY],
    )


def run_temporal(hid, dmix, wq):
    return call(
        temporal,
        [((SEQ, POS, D), BF), ((SEQ, POS, D), BF)],
        (hid, dmix, wq),
        [WIDE, TOK, TOK, TOK3, TOK, TOK3, SLOTS, SLOTS, SLOTS, SLOTS, DMA((4,))],
        8 * UNIT,
        [VMEM, VMEM, ANY],
    )


def run_spatial_backward(dhid, stream, gt, og, qkv, prob, clip, gs, wo, wq):
    return call(
        spatial_backward,
        [((T, D), BF)],
        (dhid, stream, gt, og, qkv, prob, clip, gs, wo, wq),
        [TOK, TOKF, TOK, TOK3, PROB, TOK, SQUARE, WIDE, TOKF, TOK, TOK, TOK3, TOK,
         SLOTS, SLOTS, SLOTS, DMA((8,))],
        7 * UNIT,
        [ANY, ANY, VMEM, ANY, ANY, ANY, ANY, VMEM, ANY, ANY],
    )[0]


def run_outer_product(core, mixed, other_mixed, og, other_og):
    pair = VMEM((2 * T, D), BF)
    return call(
        outer_product,
        [((GROUPS * SEQ, CHUNK, LANES), BF)],
        (core, mixed, other_mixed, og, other_og),
        [pair, pair, VMEM((D, D), F32), DMA((4,))],
        2 * UNIT,
        [pltpu.SMEM, ANY, ANY, ANY, ANY],
    )[0]


def run_sum_chunks(owner, parts, scale):
    def finish(owner_ref, got_ref, out_ref, total_ref):
        sum_chunks(owner_ref, got_ref, out_ref, total_ref, scale=scale)

    return call(
        finish,
        [((OWN, D), F32)],
        (owner, parts),
        [VMEM((CHUNK, LANES), F32)],
        1000,
        [pltpu.SMEM, VMEM],
    )[0]


def per_device(
    video,
    out_grad,
    gain_spatial,
    gain_temporal,
    w_spatial_qkv,
    w_spatial_out,
    w_temporal_qkv,
    w_temporal_out,
):
    tokens = lax.axis_size("dp") * video.shape[0] * SEQ * T
    shape = video.shape
    clip = video.reshape(T, D)
    og = out_grad.reshape(T, D)

    def exchange(x):
        return lax.all_to_all(x.reshape(SEQ, POS, D), "seq", 0, 0, tiled=True)

    def swap(x):
        return lax.ppermute(x, "dp", [(i, i ^ 1) for i in range(DP)])

    og_pos = exchange(og)
    other_og = swap(og_pos)
    hid, stream, qkv, prob = run_spatial_forward(
        clip, gain_spatial, gain_temporal, w_spatial_qkv, w_spatial_out
    )
    hid_pos = exchange(hid)
    dmix = nt(og_pos.reshape(T, D), w_temporal_out).astype(BF).reshape(SEQ, POS, D)
    mixed_pos, dhid_pos = run_temporal(hid_pos, dmix, w_temporal_qkv)
    dhid = exchange(dhid_pos).reshape(T, D)

    core = lax.rem(lax.axis_index("dp"), 2).reshape(1)
    other_mixed = swap(mixed_pos)
    chunks = run_outer_product(
        core, *(x.reshape(T, D) for x in (mixed_pos, other_mixed, og_pos, other_og))
    )
    chunks, dhid = lax.optimization_barrier((chunks, dhid))
    owners = [
        [(g * 2 + c) * SEQ + s for g in range(GROUPS) for s in range(SEQ)] for c in range(2)
    ]
    parts = lax.all_to_all(
        chunks, ("dp", "seq"), 0, 0, axis_index_groups=owners, tiled=True
    )
    video_grad = run_spatial_backward(
        dhid, stream, gain_temporal, og, qkv, prob, clip, gain_spatial,
        w_spatial_out, w_spatial_qkv,
    )
    owner = lax.axis_index("seq").reshape(1)
    w_grad = run_sum_chunks(owner, parts, 1.0 / math.sqrt(float(tokens)))
    return (video_grad.reshape(shape), w_grad)


def solution(mesh):
    return jax.shard_map(
        per_device,
        mesh=mesh,
        in_specs=(
            P("dp", "seq", None, None),
            P("dp", "seq", None, None),
            P(),
            P(),
            P(),
            P(),
            P(),
            P(),
        ),
        out_specs=(P("dp", "seq", None, None), P(("dp", "seq"), None)),
        check_vma=False,
    )
```

```python
import math

import jax
import jax.numpy as jnp
from jax import lax
from jax.experimental import pallas as pl
from jax.experimental.pallas import tpu as pltpu
from jax.sharding import PartitionSpec as P


HEADS = 16
D = 1152
HD = D // HEADS
T = 256
SEQ = 8
POS = T // SEQ
DP = 16
EPS = 1e-06
LOG2E = 1.0 / math.log(2.0)
SCALE = 1.0 / math.sqrt(HD)
BF = jnp.bfloat16
F32 = jnp.float32
ROWS = 32
WIN = 256
CHUNK = 88
OWN = D // (DP * SEQ)
LANES = 128
TILES = D // LANES

VMEM = pltpu.VMEM
ANY = pl.ANY


def nn(a, b):
    return lax.dot_general(a, b, (((1,), (0,)), ((), ())), preferred_element_type=F32)


def nt(a, b):
    return lax.dot_general(a, b, (((1,), (1,)), ((), ())), preferred_element_type=F32)


def tn(a, b):
    return lax.dot_general(a, b, (((0,), (0,)), ((), ())), preferred_element_type=F32)


def row_stats(x):
    center = jnp.mean(x, axis=-1, keepdims=True)
    centered = x - center
    spread = jnp.mean(centered * centered, axis=-1, keepdims=True)
    return centered, lax.rsqrt(spread + EPS)


def row_blocks(fn):
    def body(i, carry):
        fn(pl.ds(pl.multiple_of(i * ROWS, ROWS), ROWS))
        return carry

    lax.fori_loop(0, T // ROWS, body, 0, unroll=4)


def norm_back(x, g, dy):
    centered, inv = row_stats(x)
    xhat = centered * inv
    dxhat = dy * g
    mean_d = jnp.mean(dxhat, axis=-1, keepdims=True)
    mean_dx = jnp.mean(dxhat * xhat, axis=-1, keepdims=True)
    return inv * (dxhat - mean_d - xhat * mean_dx)


def window(h):
    tile = jnp.minimum(lax.div(h * HD, LANES), TILES - 2)
    low = pl.multiple_of(tile * LANES, LANES)
    start = h * HD - low
    lane = lax.broadcasted_iota(jnp.int32, (1, WIN), 1)
    inside = jnp.where((lane >= start) & (lane < start + HD), 1.0, 0.0)
    return low, inside.astype(BF)


def softmax_keys(scores):
    top = jnp.max(scores, axis=0, keepdims=True)
    e = jnp.exp2((scores - top) * (SCALE * LOG2E))
    return e * (1.0 / jnp.sum(e, axis=0, keepdims=True))


def score_grad(prob, prob_grad):
    t = prob * prob_grad
    delta = jnp.sum(t, axis=0, keepdims=True)
    return ((t - prob * delta) * SCALE).astype(BF)


def heads_loop(first, second, unroll=8, ahead=1):
    def body(i, carry):
        waiting = []
        for u in range(unroll):
            h = i * unroll + u
            waiting.append((h, first(h)))
            if len(waiting) > ahead:
                h, values = waiting.pop(0)
                second(h, *values)
        for h, values in waiting:
            second(h, *values)
        return carry

    lax.fori_loop(0, HEADS // unroll, body, 0)


def merge(slots, dst, base=0):
    for t in range(TILES):
        total = None
        for h in range(HEADS):
            first = min(h * HD // LANES, TILES - 2)
            if h * HD < (t + 1) * LANES and (h + 1) * HD > t * LANES:
                at = (t - first) * LANES
                piece = slots[h, :, at : at + LANES]
                total = piece if total is None else total + piece
        dst[:, base + t * LANES : base + (t + 1) * LANES] = total


def project_back(slots, grad, weight):
    total = None
    for i, section in enumerate(slots):
        merge(section, grad, i * D)
        cols = slice(i * D, (i + 1) * D)
        part = nt(grad[:, cols], weight[:, cols])
        total = part if total is None else total + part
    return total


def fetch(src, dst, sem):
    copy = pltpu.make_async_copy(src, dst, sem)
    copy.start()
    return copy


CUTS = (0, 512, 1536, 2560, 3456)
PIECES = [slice(a, b) for a, b in zip(CUTS, CUTS[1:])]


def fetch_columns(src, dst, sems):
    return [fetch(src.at[:, p], dst.at[:, p], sems.at[i]) for i, p in enumerate(PIECES)]


def spatial_forward(video, gs, gt, wq_hbm, wo_hbm, hid_out, stream_hbm, qkv_hbm, prob_hbm,
                    wq, wo, hid, mix, stream, qkv, prob, slots, sems, out_sems):
    wq_copies = fetch_columns(wq_hbm, wq, sems)
    wo_copy = fetch(wo_hbm, wo, sems.at[4])

    def first_norm(rows):
        centered, inv = row_stats(video[rows, :].astype(F32))
        hid[rows, :] = (centered * inv * gs[...].reshape(1, D)).astype(BF)

    row_blocks(first_norm)
    for copy, p in zip(wq_copies, PIECES):
        copy.wait()
        qkv[:, p] = nn(hid[...], wq[:, p]).astype(BF)
    qkv_copy = fetch(qkv, qkv_hbm, out_sems.at[0])

    def head(h):
        low, inside = window(h)
        q = qkv[:, pl.ds(low, WIN)] * inside
        k = qkv[:, pl.ds(D + low, WIN)]
        v = qkv[:, pl.ds(2 * D + low, WIN)] * inside
        return nt(k, q), v

    def rest(h, scores, v):
        p = softmax_keys(scores).astype(BF)
        prob[h] = p
        slots[h] = tn(p, v).astype(BF)

    heads_loop(head, rest)
    prob_copy = fetch(prob, prob_hbm, out_sems.at[1])
    merge(slots, mix)
    wo_copy.wait()
    stream[...] = video[...].astype(F32) + nn(mix[...], wo[...])
    stream_copy = fetch(stream, stream_hbm, out_sems.at[2])

    def second_norm(rows):
        centered, inv = row_stats(stream[rows, :])
        hid_out[rows, :] = (centered * inv * gt[...].reshape(1, D)).astype(BF)

    row_blocks(second_norm)
    for copy in (qkv_copy, prob_copy, stream_copy):
        copy.wait()


HALF = POS // 2
BLK = SEQ * HALF


def temporal(hid_in, dmix_in, wq_hbm, mixed_out, dhid_out,
             wq, hid, dmix, qkv, mix, dqkv, dh, o_slots, q_slots, k_slots, v_slots, sems):
    wq_copies = fetch_columns(wq_hbm, wq, sems)
    for b in range(2):
        part = slice(b * HALF, (b + 1) * HALF)
        rows = slice(b * BLK, (b + 1) * BLK)
        hid[rows, :] = hid_in[:, part, :].reshape(BLK, D)
        dmix[rows, :] = dmix_in[:, part, :].reshape(BLK, D)
    for copy, p in zip(wq_copies, PIECES):
        copy.wait()
        qkv[:, p] = nn(hid[...], wq[:, p]).astype(BF)

    key_pos = lax.rem(lax.broadcasted_iota(jnp.int32, (BLK, BLK), 0), HALF)
    query_pos = lax.rem(lax.broadcasted_iota(jnp.int32, (BLK, BLK), 1), HALF)
    same = key_pos == query_pos

    def head(h):
        low, inside = window(h)
        values = []
        for b in range(2):
            rows = slice(b * BLK, (b + 1) * BLK)
            qs, ks, vs = pl.ds(low, WIN), pl.ds(D + low, WIN), pl.ds(2 * D + low, WIN)
            q = qkv[rows, qs] * inside
            k = qkv[rows, ks] * inside
            v = qkv[rows, vs] * inside
            do = dmix[rows, qs] * inside
            values.append((nt(k, q), nt(v, do), q, k, v, do))
        return values

    def rest(h, *values):
        for b, (scores, prob_grad, q, k, v, do) in enumerate(values):
            rows = slice(b * BLK, (b + 1) * BLK)
            p = softmax_keys(jnp.where(same, scores, -1e30))
            pb = p.astype(BF)
            ds = score_grad(p, prob_grad)
            o_slots[h, rows, :] = tn(pb, v).astype(BF)
            v_slots[h, rows, :] = nn(pb, do).astype(BF)
            k_slots[h, rows, :] = nn(ds, q).astype(BF)
            q_slots[h, rows, :] = tn(ds, k).astype(BF)

    heads_loop(head, rest)
    merge(o_slots, mix)
    dh[...] = project_back((q_slots, k_slots, v_slots), dqkv, wq).astype(BF)
    for b in range(2):
        part = slice(b * HALF, (b + 1) * HALF)
        rows = slice(b * BLK, (b + 1) * BLK)
        mixed_out[:, part, :] = mix[rows, :].reshape(SEQ, HALF, D)
        dhid_out[:, part, :] = dh[rows, :].reshape(SEQ, HALF, D)


def spatial_backward(dhid_hbm, stream_hbm, gt, og_hbm, qkv_hbm, prob_hbm, video_hbm, gs,
                     wo_hbm, wq_hbm, out, dhid, stream, og, qkv, prob, video, wo, wq,
                     sg, sgb, dmix, dqkv, dh, q_slots, k_slots, v_slots, sems):
    pairs = (
        (dhid_hbm, dhid), (stream_hbm, stream), (og_hbm, og), (wo_hbm, wo), (qkv_hbm, qkv),
        (prob_hbm, prob), (wq_hbm, wq), (video_hbm, video),
    )
    copies = [fetch(src, dst, sems.at[i]) for i, (src, dst) in enumerate(pairs)]
    for copy in copies[:3]:
        copy.wait()

    def stream_grad(rows):
        dx = norm_back(stream[rows, :], gt[...].reshape(1, D), dhid[rows, :].astype(F32))
        total = og[rows, :].astype(F32) + dx
        sg[rows, :] = total
        sgb[rows, :] = total.astype(BF)

    row_blocks(stream_grad)
    copies[3].wait()
    dmix[...] = nt(sgb[...], wo[...]).astype(BF)
    copies[4].wait()
    copies[5].wait()

    def head(h):
        low, inside = window(h)
        qs, ks, vs = pl.ds(low, WIN), pl.ds(D + low, WIN), pl.ds(2 * D + low, WIN)
        q = qkv[:, qs] * inside
        k = qkv[:, ks] * inside
        v = qkv[:, vs]
        do = dmix[:, qs] * inside
        return nt(v, do), q, k, do

    def rest(h, prob_grad, q, k, do):
        pb = prob[h]
        ds = score_grad(pb.astype(F32), prob_grad)
        v_slots[h] = nn(pb, do).astype(BF)
        k_slots[h] = nn(ds, q).astype(BF)
        q_slots[h] = tn(ds, k).astype(BF)

    heads_loop(head, rest)
    copies[6].wait()
    dh[...] = project_back((q_slots, k_slots, v_slots), dqkv, wq).astype(BF)
    copies[7].wait()

    def video_grad(rows):
        dx = norm_back(video[rows, :].astype(F32), gs[...].reshape(1, D), dh[rows, :].astype(F32))
        out[rows, :] = (sg[rows, :] + dx).astype(BF)

    row_blocks(video_grad)


GROUPS = DP // 2


SUB = 8


def outer_product(core, mixed, other_mixed, og, other_og, out, m, g, full, sems):
    copies = [
        fetch(mixed, m.at[:T, :], sems.at[0]),
        fetch(og, g.at[:T, :], sems.at[1]),
        fetch(other_mixed, m.at[T:, :], sems.at[2]),
        fetch(other_og, g.at[T:, :], sems.at[3]),
    ]
    for copy in copies:
        copy.wait()
    step = 3 * LANES
    for c in range(D // step):
        full[c * step : (c + 1) * step, :] = tn(m[:, c * step : (c + 1) * step], g[...])
    place = lax.broadcasted_iota(jnp.int32, (SUB, 1), 0)

    def body(i, carry):
        base = (2 * i + core[0]) * HD
        for j in range(SEQ):
            at = base + j * SUB
            upper = full[pl.ds(pl.multiple_of(at, SUB), SUB), :]
            lower = full[pl.ds(pl.multiple_of(at + SUB, SUB), SUB), :]
            eight = jnp.where(place >= j, upper, lower)
            ninth = lower[j : j + 1, :]
            parts = [eight[:, t * LANES : (t + 1) * LANES] for t in range(TILES)]
            for first in (0, SUB):
                rest = jnp.zeros((SUB, LANES), F32)
                for t in range(first, min(first + SUB, TILES)):
                    rest = jnp.where(
                        place == t - first, ninth[:, t * LANES : (t + 1) * LANES], rest
                    )
                parts.append(rest)
            out[i * SEQ + j] = jnp.concatenate(parts).astype(BF)
        return carry

    lax.fori_loop(0, GROUPS, body, 0)


def sum_chunks(owner, got, out, total, *, scale):
    total[...] = jnp.sum(got[...].astype(F32), axis=0) * scale
    back = lax.rem(SUB - owner[0], SUB)
    for t in range(TILES):
        lanes = slice(t * LANES, (t + 1) * LANES)
        out[:SUB, lanes] = pltpu.roll(total[t * SUB : (t + 1) * SUB, :], back, 0)
        out[SUB:, lanes] = total[TILES * SUB + t : TILES * SUB + t + 1, :]


def call(fn, outs, args, scratch, flops, specs=None, out_specs=None):
    if specs is None:
        specs = [VMEM] * len(args)
    if out_specs is None:
        out_specs = [VMEM] * len(outs)
    moved = sum(a.size * a.dtype.itemsize for a in args)
    moved += sum(math.prod(s) * jnp.dtype(d).itemsize for s, d in outs)
    return pl.pallas_call(
        fn,
        out_shape=[jax.ShapeDtypeStruct(s, d) for s, d in outs],
        in_specs=[pl.BlockSpec(memory_space=s) for s in specs],
        out_specs=[pl.BlockSpec(memory_space=s) for s in out_specs],
        scratch_shapes=scratch,
        cost_estimate=pl.CostEstimate(flops=flops, bytes_accessed=moved, transcendentals=0),
    )(*args)


UNIT = 2 * T * D * D
WIDE, SQUARE = VMEM((D, 3 * D), BF), VMEM((D, D), BF)
TOK, TOK3, TOKF = VMEM((T, D), BF), VMEM((T, 3 * D), BF), VMEM((T, D), F32)
PROB, SLOTS = VMEM((HEADS, T, T), BF), VMEM((HEADS, T, WIN), BF)
DMA = pltpu.SemaphoreType.DMA


def run_spatial_forward(clip, gs, gt, wq, wo):
    return call(
        spatial_forward,
        [((T, D), BF), ((T, D), F32), ((T, 3 * D), BF), ((HEADS, T, T), BF)],
        (clip, gs, gt, wq, wo),
        [WIDE, SQUARE, TOK, TOK, TOKF, TOK3, PROB, SLOTS, DMA((5,)), DMA((3,))],
        5 * UNIT,
        [VMEM, VMEM, VMEM, ANY, ANY],
        [VMEM, ANY, ANY, ANY],
    )


def run_temporal(hid, dmix, wq):
    return call(
        temporal,
        [((SEQ, POS, D), BF), ((SEQ, POS, D), BF)],
        (hid, dmix, wq),
        [WIDE, TOK, TOK, TOK3, TOK, TOK3, TOK, SLOTS, SLOTS, SLOTS, SLOTS, DMA((4,))],
        8 * UNIT,
        [VMEM, VMEM, ANY],
    )


def run_spatial_backward(dhid, stream, gt, og, qkv, prob, clip, gs, wo, wq):
    return call(
        spatial_backward,
        [((T, D), BF)],
        (dhid, stream, gt, og, qkv, prob, clip, gs, wo, wq),
        [TOK, TOKF, TOK, TOK3, PROB, TOK, SQUARE, WIDE, TOKF, TOK, TOK, TOK3, TOK,
         SLOTS, SLOTS, SLOTS, DMA((8,))],
        7 * UNIT,
        [ANY, ANY, VMEM, ANY, ANY, ANY, ANY, VMEM, ANY, ANY],
    )[0]


def run_outer_product(core, mixed, other_mixed, og, other_og):
    pair = VMEM((2 * T, D), BF)
    return call(
        outer_product,
        [((GROUPS * SEQ, CHUNK, LANES), BF)],
        (core, mixed, other_mixed, og, other_og),
        [pair, pair, VMEM((D, D), F32), DMA((4,))],
        2 * UNIT,
        [pltpu.SMEM, ANY, ANY, ANY, ANY],
    )[0]


def run_sum_chunks(owner, parts, scale):
    def finish(owner_ref, got_ref, out_ref, total_ref):
        sum_chunks(owner_ref, got_ref, out_ref, total_ref, scale=scale)

    return call(
        finish,
        [((OWN, D), F32)],
        (owner, parts),
        [VMEM((CHUNK, LANES), F32)],
        1000,
        [pltpu.SMEM, VMEM],
    )[0]


def per_device(
    video,
    out_grad,
    gain_spatial,
    gain_temporal,
    w_spatial_qkv,
    w_spatial_out,
    w_temporal_qkv,
    w_temporal_out,
):
    tokens = lax.axis_size("dp") * video.shape[0] * SEQ * T
    shape = video.shape
    clip = video.reshape(T, D)
    og = out_grad.reshape(T, D)

    def exchange(x):
        return lax.all_to_all(x.reshape(SEQ, POS, D), "seq", 0, 0, tiled=True)

    def swap(x):
        return lax.ppermute(x, "dp", [(i, i ^ 1) for i in range(DP)])

    og_pos = exchange(og)
    other_og = swap(og_pos)
    hid, stream, qkv, prob = run_spatial_forward(
        clip, gain_spatial, gain_temporal, w_spatial_qkv, w_spatial_out
    )
    hid_pos = exchange(hid)
    dmix = nt(og_pos.reshape(T, D), w_temporal_out).astype(BF).reshape(SEQ, POS, D)
    mixed_pos, dhid_pos = run_temporal(hid_pos, dmix, w_temporal_qkv)
    dhid = exchange(dhid_pos).reshape(T, D)

    core = lax.rem(lax.axis_index("dp"), 2).reshape(1)
    other_mixed = swap(mixed_pos)
    chunks = run_outer_product(
        core, *(x.reshape(T, D) for x in (mixed_pos, other_mixed, og_pos, other_og))
    )
    chunks, dhid = lax.optimization_barrier((chunks, dhid))
    owners = [
        [(g * 2 + c) * SEQ + s for g in range(GROUPS) for s in range(SEQ)] for c in range(2)
    ]
    parts = lax.all_to_all(
        chunks, ("dp", "seq"), 0, 0, axis_index_groups=owners, tiled=True
    )
    video_grad = run_spatial_backward(
        dhid, stream, gain_temporal, og, qkv, prob, clip, gain_spatial,
        w_spatial_out, w_spatial_qkv,
    )
    owner = lax.axis_index("seq").reshape(1)
    w_grad = run_sum_chunks(owner, parts, 1.0 / math.sqrt(float(tokens)))
    return (video_grad.reshape(shape), w_grad)


def solution(mesh):
    return jax.shard_map(
        per_device,
        mesh=mesh,
        in_specs=(
            P("dp", "seq", None, None),
            P("dp", "seq", None, None),
            P(),
            P(),
            P(),
            P(),
            P(),
            P(),
        ),
        out_specs=(P("dp", "seq", None, None), P(("dp", "seq"), None)),
        check_vma=False,
    )
```

```python
import math

import jax
import jax.numpy as jnp
from jax import lax
from jax.experimental import pallas as pl
from jax.experimental.pallas import tpu as pltpu
from jax.sharding import PartitionSpec as P


HEADS = 16
D = 1152
HD = D // HEADS
T = 256
SEQ = 8
POS = T // SEQ
DP = 16
EPS = 1e-06
LOG2E = 1.0 / math.log(2.0)
SCALE = 1.0 / math.sqrt(HD)
BF = jnp.bfloat16
F32 = jnp.float32
ROWS = 32
WIN = 256
CHUNK = 88
OWN = D // (DP * SEQ)
LANES = 128
TILES = D // LANES

VMEM = pltpu.VMEM
ANY = pl.ANY


def nn(a, b):
    return lax.dot_general(a, b, (((1,), (0,)), ((), ())), preferred_element_type=F32)


def nt(a, b):
    return lax.dot_general(a, b, (((1,), (1,)), ((), ())), preferred_element_type=F32)


def tn(a, b):
    return lax.dot_general(a, b, (((0,), (0,)), ((), ())), preferred_element_type=F32)


def row_stats(x):
    center = jnp.mean(x, axis=-1, keepdims=True)
    centered = x - center
    spread = jnp.mean(centered * centered, axis=-1, keepdims=True)
    return centered, lax.rsqrt(spread + EPS)


def row_blocks(fn):
    def body(i, carry):
        fn(pl.ds(pl.multiple_of(i * ROWS, ROWS), ROWS))
        return carry

    lax.fori_loop(0, T // ROWS, body, 0, unroll=4)


def norm_back(x, g, dy):
    centered, inv = row_stats(x)
    xhat = centered * inv
    dxhat = dy * g
    mean_d = jnp.mean(dxhat, axis=-1, keepdims=True)
    mean_dx = jnp.mean(dxhat * xhat, axis=-1, keepdims=True)
    return inv * (dxhat - mean_d - xhat * mean_dx)


def window(h):
    low = h * HD // LANES * LANES
    width = -(-(h * HD + HD - low) // LANES) * LANES
    start = h * HD - low
    lane = lax.broadcasted_iota(jnp.int32, (1, width), 1)
    inside = jnp.where((lane >= start) & (lane < start + HD), 1.0, 0.0)
    return low, width, inside.astype(BF)


def softmax_keys(scores):
    top = jnp.max(scores, axis=0, keepdims=True)
    e = jnp.exp2((scores - top) * (SCALE * LOG2E))
    return e * (1.0 / jnp.sum(e, axis=0, keepdims=True))


def score_grad(prob, prob_grad):
    t = prob * prob_grad
    delta = jnp.sum(t, axis=0, keepdims=True)
    return ((t - prob * delta) * SCALE).astype(BF)


def all_heads(first, second):
    waiting = None
    for h in range(HEADS):
        values = first(h)
        if waiting is not None:
            second(h - 1, *waiting)
        waiting = values
    second(HEADS - 1, *waiting)


def merge(slots, dst, base=0):
    for t in range(TILES):
        total = None
        for h in range(HEADS):
            if h * HD < (t + 1) * LANES and (h + 1) * HD > t * LANES:
                at = (t - h * HD // LANES) * LANES
                piece = slots[h, :, at : at + LANES]
                total = piece if total is None else total + piece
        dst[:, base + t * LANES : base + (t + 1) * LANES] = total


def project_back(slots, grad, weight):
    total = None
    for i, section in enumerate(slots):
        merge(section, grad, i * D)
        cols = slice(i * D, (i + 1) * D)
        part = nt(grad[:, cols], weight[:, cols])
        total = part if total is None else total + part
    return total


def fetch(src, dst, sem):
    copy = pltpu.make_async_copy(src, dst, sem)
    copy.start()
    return copy


CUTS = (0, 512, 1536, 2560, 3456)
PIECES = [slice(a, b) for a, b in zip(CUTS, CUTS[1:])]


def fetch_columns(src, dst, sems):
    return [fetch(src.at[:, p], dst.at[:, p], sems.at[i]) for i, p in enumerate(PIECES)]


def spatial_forward(video, gs, gt, wq_hbm, wo_hbm, hid_out, mix_hbm, qkv_hbm, prob_hbm,
                    wq, wo, hid, mix, stream, qkv, prob, slots, sems, out_sems):
    wq_copies = fetch_columns(wq_hbm, wq, sems)
    wo_copy = fetch(wo_hbm, wo, sems.at[4])

    def first_norm(rows):
        centered, inv = row_stats(video[rows, :].astype(F32))
        hid[rows, :] = (centered * inv * gs[...].reshape(1, D)).astype(BF)

    row_blocks(first_norm)
    for copy, p in zip(wq_copies, PIECES):
        copy.wait()
        qkv[:, p] = nn(hid[...], wq[:, p]).astype(BF)
    qkv_copy = fetch(qkv, qkv_hbm, out_sems.at[0])

    def head(h):
        low, width, inside = window(h)
        q = qkv[:, pl.ds(low, width)] * inside
        k = qkv[:, pl.ds(D + low, width)]
        v = qkv[:, pl.ds(2 * D + low, width)] * inside
        return nt(k, q), v

    def rest(h, scores, v):
        p = softmax_keys(scores).astype(BF)
        prob[h] = p
        slots[h, :, : v.shape[1]] = tn(p, v).astype(BF)

    all_heads(head, rest)
    prob_copy = fetch(prob, prob_hbm, out_sems.at[1])
    merge(slots, mix)
    mix_copy = fetch(mix, mix_hbm, out_sems.at[2])
    wo_copy.wait()
    stream[...] = video[...].astype(F32) + nn(mix[...], wo[...])

    def second_norm(rows):
        centered, inv = row_stats(stream[rows, :])
        hid_out[rows, :] = (centered * inv * gt[...].reshape(1, D)).astype(BF)

    row_blocks(second_norm)
    for copy in (qkv_copy, prob_copy, mix_copy):
        copy.wait()


HALF = POS // 2
BLK = SEQ * HALF


def temporal(hid_in, dmix_in, wq_hbm, mixed_out, dhid_out,
             wq, hid, dmix, qkv, mix, dqkv, dh, o_slots, q_slots, k_slots, v_slots, sems):
    wq_copies = fetch_columns(wq_hbm, wq, sems)
    for b in range(2):
        part = slice(b * HALF, (b + 1) * HALF)
        rows = slice(b * BLK, (b + 1) * BLK)
        hid[rows, :] = hid_in[:, part, :].reshape(BLK, D)
        dmix[rows, :] = dmix_in[:, part, :].reshape(BLK, D)
    for copy, p in zip(wq_copies, PIECES):
        copy.wait()
        qkv[:, p] = nn(hid[...], wq[:, p]).astype(BF)

    key_pos = lax.rem(lax.broadcasted_iota(jnp.int32, (BLK, BLK), 0), HALF)
    query_pos = lax.rem(lax.broadcasted_iota(jnp.int32, (BLK, BLK), 1), HALF)
    same = key_pos == query_pos

    def head(h):
        low, width, inside = window(h)
        values = []
        for b in range(2):
            rows = slice(b * BLK, (b + 1) * BLK)
            qs, ks, vs = pl.ds(low, width), pl.ds(D + low, width), pl.ds(2 * D + low, width)
            q = qkv[rows, qs] * inside
            k = qkv[rows, ks] * inside
            v = qkv[rows, vs] * inside
            do = dmix[rows, qs] * inside
            values.append((nt(k, q), nt(v, do), q, k, v, do))
        return values

    def rest(h, *values):
        for b, (scores, prob_grad, q, k, v, do) in enumerate(values):
            rows = slice(b * BLK, (b + 1) * BLK)
            p = softmax_keys(jnp.where(same, scores, -1e30))
            pb = p.astype(BF)
            ds = score_grad(p, prob_grad)
            o_slots[h, rows, : q.shape[1]] = tn(pb, v).astype(BF)
            v_slots[h, rows, : q.shape[1]] = nn(pb, do).astype(BF)
            k_slots[h, rows, : q.shape[1]] = nn(ds, q).astype(BF)
            q_slots[h, rows, : q.shape[1]] = tn(ds, k).astype(BF)

    all_heads(head, rest)
    merge(o_slots, mix)
    dh[...] = project_back((q_slots, k_slots, v_slots), dqkv, wq).astype(BF)
    for b in range(2):
        part = slice(b * HALF, (b + 1) * HALF)
        rows = slice(b * BLK, (b + 1) * BLK)
        mixed_out[:, part, :] = mix[rows, :].reshape(SEQ, HALF, D)
        dhid_out[:, part, :] = dh[rows, :].reshape(SEQ, HALF, D)


def spatial_backward(dhid_hbm, mix_hbm, gt, og_hbm, qkv_hbm, prob_hbm, video_hbm, gs,
                     wo_hbm, wq_hbm, out, dhid, mix, stream, og, qkv, prob, video, wo, wq,
                     sg, sgb, dmix, dqkv, dh, q_slots, k_slots, v_slots, sems):
    pairs = (
        (wo_hbm, wo), (mix_hbm, mix), (video_hbm, video), (dhid_hbm, dhid), (og_hbm, og),
        (qkv_hbm, qkv), (prob_hbm, prob), (wq_hbm, wq),
    )
    copies = [fetch(src, dst, sems.at[i]) for i, (src, dst) in enumerate(pairs)]
    for copy in copies[:3]:
        copy.wait()
    stream[...] = video[...].astype(F32) + nn(mix[...], wo[...])
    for copy in copies[3:5]:
        copy.wait()

    def stream_grad(rows):
        dx = norm_back(stream[rows, :], gt[...].reshape(1, D), dhid[rows, :].astype(F32))
        total = og[rows, :].astype(F32) + dx
        sg[rows, :] = total
        sgb[rows, :] = total.astype(BF)

    row_blocks(stream_grad)
    dmix[...] = nt(sgb[...], wo[...]).astype(BF)
    copies[5].wait()
    copies[6].wait()

    def head(h):
        low, width, inside = window(h)
        qs, ks, vs = pl.ds(low, width), pl.ds(D + low, width), pl.ds(2 * D + low, width)
        q = qkv[:, qs] * inside
        k = qkv[:, ks] * inside
        v = qkv[:, vs]
        do = dmix[:, qs] * inside
        return nt(v, do), q, k, do

    def rest(h, prob_grad, q, k, do):
        pb = prob[h]
        ds = score_grad(pb.astype(F32), prob_grad)
        v_slots[h, :, : q.shape[1]] = nn(pb, do).astype(BF)
        k_slots[h, :, : q.shape[1]] = nn(ds, q).astype(BF)
        q_slots[h, :, : q.shape[1]] = tn(ds, k).astype(BF)

    all_heads(head, rest)
    copies[7].wait()
    dh[...] = project_back((q_slots, k_slots, v_slots), dqkv, wq).astype(BF)

    def video_grad(rows):
        dx = norm_back(video[rows, :].astype(F32), gs[...].reshape(1, D), dh[rows, :].astype(F32))
        out[rows, :] = (sg[rows, :] + dx).astype(BF)

    row_blocks(video_grad)


GROUPS = DP // 2


SUB = 8


def outer_product(core, mixed, other_mixed, og, other_og, out, m, g, full, sems):
    copies = [
        fetch(mixed, m.at[:T, :], sems.at[0]),
        fetch(og, g.at[:T, :], sems.at[1]),
        fetch(other_mixed, m.at[T:, :], sems.at[2]),
        fetch(other_og, g.at[T:, :], sems.at[3]),
    ]
    for copy in copies:
        copy.wait()
    step = 3 * LANES
    for c in range(D // step):
        full[c * step : (c + 1) * step, :] = tn(m[:, c * step : (c + 1) * step], g[...])
    place = lax.broadcasted_iota(jnp.int32, (SUB, 1), 0)

    def body(i, carry):
        base = (2 * i + core[0]) * HD
        for j in range(SEQ):
            at = base + j * SUB
            upper = full[pl.ds(pl.multiple_of(at, SUB), SUB), :]
            lower = full[pl.ds(pl.multiple_of(at + SUB, SUB), SUB), :]
            eight = jnp.where(place >= j, upper, lower)
            ninth = lower[j : j + 1, :]
            parts = [eight[:, t * LANES : (t + 1) * LANES] for t in range(TILES)]
            for first in (0, SUB):
                rest = jnp.zeros((SUB, LANES), F32)
                for t in range(first, min(first + SUB, TILES)):
                    rest = jnp.where(
                        place == t - first, ninth[:, t * LANES : (t + 1) * LANES], rest
                    )
                parts.append(rest)
            out[i * SEQ + j] = jnp.concatenate(parts).astype(BF)
        return carry

    lax.fori_loop(0, GROUPS, body, 0)


def sum_chunks(owner, got, out, total, *, scale):
    total[...] = jnp.sum(got[...].astype(F32), axis=0) * scale
    back = lax.rem(SUB - owner[0], SUB)
    for t in range(TILES):
        lanes = slice(t * LANES, (t + 1) * LANES)
        out[:SUB, lanes] = pltpu.roll(total[t * SUB : (t + 1) * SUB, :], back, 0)
        out[SUB:, lanes] = total[TILES * SUB + t : TILES * SUB + t + 1, :]


def call(fn, outs, args, scratch, flops, specs=None, out_specs=None):
    if specs is None:
        specs = [VMEM] * len(args)
    if out_specs is None:
        out_specs = [VMEM] * len(outs)
    moved = sum(a.size * a.dtype.itemsize for a in args)
    moved += sum(math.prod(s) * jnp.dtype(d).itemsize for s, d in outs)
    return pl.pallas_call(
        fn,
        out_shape=[jax.ShapeDtypeStruct(s, d) for s, d in outs],
        in_specs=[pl.BlockSpec(memory_space=s) for s in specs],
        out_specs=[pl.BlockSpec(memory_space=s) for s in out_specs],
        scratch_shapes=scratch,
        cost_estimate=pl.CostEstimate(flops=flops, bytes_accessed=moved, transcendentals=0),
    )(*args)


UNIT = 2 * T * D * D
WIDE, SQUARE = VMEM((D, 3 * D), BF), VMEM((D, D), BF)
TOK, TOK3, TOKF = VMEM((T, D), BF), VMEM((T, 3 * D), BF), VMEM((T, D), F32)
PROB, SLOTS = VMEM((HEADS, T, T), BF), VMEM((HEADS, T, WIN), BF)
DMA = pltpu.SemaphoreType.DMA


def run_spatial_forward(clip, gs, gt, wq, wo):
    return call(
        spatial_forward,
        [((T, D), BF), ((T, D), BF), ((T, 3 * D), BF), ((HEADS, T, T), BF)],
        (clip, gs, gt, wq, wo),
        [WIDE, SQUARE, TOK, TOK, TOKF, TOK3, PROB, SLOTS, DMA((5,)), DMA((3,))],
        5 * UNIT,
        [VMEM, VMEM, VMEM, ANY, ANY],
        [VMEM, ANY, ANY, ANY],
    )


def run_temporal(hid, dmix, wq):
    return call(
        temporal,
        [((SEQ, POS, D), BF), ((SEQ, POS, D), BF)],
        (hid, dmix, wq),
        [WIDE, TOK, TOK, TOK3, TOK, TOK3, TOK, SLOTS, SLOTS, SLOTS, SLOTS, DMA((4,))],
        8 * UNIT,
        [VMEM, VMEM, ANY],
    )


def run_spatial_backward(dhid, mix, gt, og, qkv, prob, clip, gs, wo, wq):
    return call(
        spatial_backward,
        [((T, D), BF)],
        (dhid, mix, gt, og, qkv, prob, clip, gs, wo, wq),
        [TOK, TOK, TOKF, TOK, TOK3, PROB, TOK, SQUARE, WIDE, TOKF, TOK, TOK, TOK3, TOK,
         SLOTS, SLOTS, SLOTS, DMA((8,))],
        7 * UNIT,
        [ANY, ANY, VMEM, ANY, ANY, ANY, ANY, VMEM, ANY, ANY],
    )[0]


def run_outer_product(core, mixed, other_mixed, og, other_og):
    pair = VMEM((2 * T, D), BF)
    return call(
        outer_product,
        [((GROUPS * SEQ, CHUNK, LANES), BF)],
        (core, mixed, other_mixed, og, other_og),
        [pair, pair, VMEM((D, D), F32), DMA((4,))],
        2 * UNIT,
        [pltpu.SMEM, ANY, ANY, ANY, ANY],
    )[0]


def run_sum_chunks(owner, parts, scale):
    def finish(owner_ref, got_ref, out_ref, total_ref):
        sum_chunks(owner_ref, got_ref, out_ref, total_ref, scale=scale)

    return call(
        finish,
        [((OWN, D), F32)],
        (owner, parts),
        [VMEM((CHUNK, LANES), F32)],
        1000,
        [pltpu.SMEM, VMEM],
    )[0]


def per_device(
    video,
    out_grad,
    gain_spatial,
    gain_temporal,
    w_spatial_qkv,
    w_spatial_out,
    w_temporal_qkv,
    w_temporal_out,
):
    tokens = lax.axis_size("dp") * video.shape[0] * SEQ * T
    shape = video.shape
    clip = video.reshape(T, D)
    og = out_grad.reshape(T, D)

    def exchange(x):
        return lax.all_to_all(x.reshape(SEQ, POS, D), "seq", 0, 0, tiled=True)

    def swap(x):
        return lax.ppermute(x, "dp", [(i, i ^ 1) for i in range(DP)])

    og_pos = exchange(og)
    other_og = swap(og_pos)
    hid, mix, qkv, prob = run_spatial_forward(
        clip, gain_spatial, gain_temporal, w_spatial_qkv, w_spatial_out
    )
    hid_pos = exchange(hid)
    dmix = nt(og_pos.reshape(T, D), w_temporal_out).astype(BF).reshape(SEQ, POS, D)
    mixed_pos, dhid_pos = run_temporal(hid_pos, dmix, w_temporal_qkv)
    dhid = exchange(dhid_pos).reshape(T, D)

    core = lax.rem(lax.axis_index("dp"), 2).reshape(1)
    other_mixed = swap(mixed_pos)
    chunks = run_outer_product(
        core, *(x.reshape(T, D) for x in (mixed_pos, other_mixed, og_pos, other_og))
    )
    chunks, dhid = lax.optimization_barrier((chunks, dhid))
    owners = [
        [(g * 2 + c) * SEQ + s for g in range(GROUPS) for s in range(SEQ)] for c in range(2)
    ]
    parts = lax.all_to_all(
        chunks, ("dp", "seq"), 0, 0, axis_index_groups=owners, tiled=True
    )
    video_grad = run_spatial_backward(
        dhid, mix, gain_temporal, og, qkv, prob, clip, gain_spatial,
        w_spatial_out, w_spatial_qkv,
    )
    owner = lax.axis_index("seq").reshape(1)
    w_grad = run_sum_chunks(owner, parts, 1.0 / math.sqrt(float(tokens)))
    return (video_grad.reshape(shape), w_grad)


def solution(mesh):
    return jax.shard_map(
        per_device,
        mesh=mesh,
        in_specs=(
            P("dp", "seq", None, None),
            P("dp", "seq", None, None),
            P(),
            P(),
            P(),
            P(),
            P(),
            P(),
        ),
        out_specs=(P("dp", "seq", None, None), P(("dp", "seq"), None)),
        check_vma=False,
    )
```

```python
import math

import jax
import jax.numpy as jnp
from jax import lax
from jax.experimental import pallas as pl
from jax.experimental.pallas import tpu as pltpu
from jax.sharding import PartitionSpec as P


HEADS = 16
D = 1152
HD = D // HEADS
T = 256
SEQ = 8
POS = T // SEQ
DP = 16
EPS = 1e-06
LOG2E = 1.0 / math.log(2.0)
SCALE = 1.0 / math.sqrt(HD)
BF = jnp.bfloat16
F32 = jnp.float32
ROWS = 32
WIN = 256
CHUNK = 88
OWN = D // (DP * SEQ)
LANES = 128
TILES = D // LANES

VMEM = pltpu.VMEM
ANY = pl.ANY


def nn(a, b):
    return lax.dot_general(a, b, (((1,), (0,)), ((), ())), preferred_element_type=F32)


def nt(a, b):
    return lax.dot_general(a, b, (((1,), (1,)), ((), ())), preferred_element_type=F32)


def tn(a, b):
    return lax.dot_general(a, b, (((0,), (0,)), ((), ())), preferred_element_type=F32)


def row_stats(x):
    center = jnp.mean(x, axis=-1, keepdims=True)
    centered = x - center
    spread = jnp.mean(centered * centered, axis=-1, keepdims=True)
    return centered, lax.rsqrt(spread + EPS)


def row_blocks(fn, first=0, last=T // ROWS):
    def body(i, carry):
        fn(pl.ds(pl.multiple_of(i * ROWS, ROWS), ROWS))
        return carry

    lax.fori_loop(first, last, body, 0, unroll=4)


def norm_back(x, g, dy):
    centered, inv = row_stats(x)
    xhat = centered * inv
    dxhat = dy * g
    mean_d = jnp.mean(dxhat, axis=-1, keepdims=True)
    mean_dx = jnp.mean(dxhat * xhat, axis=-1, keepdims=True)
    return inv * (dxhat - mean_d - xhat * mean_dx)


def window(h):
    low = h * HD // LANES * LANES
    width = -(-(h * HD + HD - low) // LANES) * LANES
    start = h * HD - low
    lane = lax.broadcasted_iota(jnp.int32, (1, width), 1)
    inside = jnp.where((lane >= start) & (lane < start + HD), 1.0, 0.0)
    return low, width, inside.astype(BF)


def softmax_keys(scores):
    top = jnp.max(scores, axis=0, keepdims=True)
    e = jnp.exp2((scores - top) * (SCALE * LOG2E))
    return e * (1.0 / jnp.sum(e, axis=0, keepdims=True))


def score_grad(prob, prob_grad):
    t = prob * prob_grad
    delta = jnp.sum(t, axis=0, keepdims=True)
    return ((t - prob * delta) * SCALE).astype(BF)


def all_heads(first, second):
    waiting = None
    for h in range(HEADS):
        values = first(h)
        if waiting is not None:
            second(h - 1, *waiting)
        waiting = values
    second(HEADS - 1, *waiting)


def merge(slots, dst, base=0):
    for t in range(TILES):
        total = None
        for h in range(HEADS):
            if h * HD < (t + 1) * LANES and (h + 1) * HD > t * LANES:
                at = (t - h * HD // LANES) * LANES
                piece = slots[h, :, at : at + LANES]
                total = piece if total is None else total + piece
        dst[:, base + t * LANES : base + (t + 1) * LANES] = total


def project_back(slots, grad, weight):
    total = None
    for i, section in enumerate(slots):
        merge(section, grad, i * D)
        cols = slice(i * D, (i + 1) * D)
        part = nt(grad[:, cols], weight[:, cols])
        total = part if total is None else total + part
    return total


def fetch(src, dst, sem):
    copy = pltpu.make_async_copy(src, dst, sem)
    copy.start()
    return copy


CUTS = (0, 512, 1536, 2560, 3456)
PIECES = [slice(a, b) for a, b in zip(CUTS, CUTS[1:])]


def fetch_columns(src, dst, sems):
    return [fetch(src.at[:, p], dst.at[:, p], sems.at[i]) for i, p in enumerate(PIECES)]


def spatial_forward(video, gs, gt, wq_hbm, wo_hbm, hid_hbm, mix_hbm, qkv_hbm, prob_hbm,
                    wq, wo, hid, mix, stream, qkv, prob, slots, sems, out_sems):
    wq_copies = fetch_columns(wq_hbm, wq, sems)
    wo_copy = fetch(wo_hbm, wo, sems.at[4])

    def first_norm(rows):
        centered, inv = row_stats(video[rows, :].astype(F32))
        hid[rows, :] = (centered * inv * gs[...].reshape(1, D)).astype(BF)

    row_blocks(first_norm)
    for copy, p in zip(wq_copies, PIECES):
        copy.wait()
        qkv[:, p] = nn(hid[...], wq[:, p]).astype(BF)
    qkv_copy = fetch(qkv, qkv_hbm, out_sems.at[0])

    def head(h):
        low, width, inside = window(h)
        q = qkv[:, pl.ds(low, width)] * inside
        k = qkv[:, pl.ds(D + low, width)]
        v = qkv[:, pl.ds(2 * D + low, width)] * inside
        return nt(k, q), v

    def rest(h, scores, v):
        p = softmax_keys(scores).astype(BF)
        prob[h] = p
        slots[h, :, : v.shape[1]] = tn(p, v).astype(BF)

    all_heads(head, rest)
    prob_copy = fetch(prob, prob_hbm, out_sems.at[1])
    merge(slots, mix)
    mix_copy = fetch(mix, mix_hbm, out_sems.at[2])
    wo_copy.wait()
    stream[...] = video[...].astype(F32) + nn(mix[...], wo[...])

    def second_norm(rows):
        centered, inv = row_stats(stream[rows, :])
        hid[rows, :] = (centered * inv * gt[...].reshape(1, D)).astype(BF)

    copies = [qkv_copy, prob_copy, mix_copy]
    for i in range(2):
        row_blocks(second_norm, i * T // ROWS // 2, (i + 1) * T // ROWS // 2)
        rows = slice(i * T // 2, (i + 1) * T // 2)
        copies.append(fetch(hid.at[rows, :], hid_hbm.at[rows, :], out_sems.at[3 + i]))
    for copy in copies:
        copy.wait()


HALF = POS // 2
BLK = SEQ * HALF


def block_of(ref, b):
    return ref.at[b * BLK : (b + 1) * BLK, :].reshape(SEQ, HALF, D)


def fetch_blocks(src, dst, sems, first):
    return [
        fetch(src.at[:, b * HALF : (b + 1) * HALF, :], block_of(dst, b), sems.at[first + b])
        for b in range(2)
    ]


def store_blocks(src, dst, sems, first):
    return [
        fetch(block_of(src, b), dst.at[:, b * HALF : (b + 1) * HALF, :], sems.at[first + b])
        for b in range(2)
    ]


def temporal(hid_hbm, dmix_hbm, wq_hbm, mixed_hbm, dhid_hbm,
             wq, hid, dmix, qkv, mix, dqkv, dh, o_slots, q_slots, k_slots, v_slots, sems, io_sems):
    hid_copies = fetch_blocks(hid_hbm, hid, io_sems, 0)
    wq_copies = fetch_columns(wq_hbm, wq, sems)
    dmix_copies = fetch_blocks(dmix_hbm, dmix, io_sems, 2)
    for copy in hid_copies:
        copy.wait()
    for copy, p in zip(wq_copies, PIECES):
        copy.wait()
        qkv[:, p] = nn(hid[...], wq[:, p]).astype(BF)
    for copy in dmix_copies:
        copy.wait()

    key_pos = lax.rem(lax.broadcasted_iota(jnp.int32, (BLK, BLK), 0), HALF)
    query_pos = lax.rem(lax.broadcasted_iota(jnp.int32, (BLK, BLK), 1), HALF)
    same = key_pos == query_pos

    def head(h):
        low, width, inside = window(h)
        values = []
        for b in range(2):
            rows = slice(b * BLK, (b + 1) * BLK)
            qs, ks, vs = pl.ds(low, width), pl.ds(D + low, width), pl.ds(2 * D + low, width)
            q = qkv[rows, qs] * inside
            k = qkv[rows, ks] * inside
            v = qkv[rows, vs] * inside
            do = dmix[rows, qs] * inside
            values.append((nt(k, q), nt(v, do), q, k, v, do))
        return values

    def rest(h, *values):
        for b, (scores, prob_grad, q, k, v, do) in enumerate(values):
            rows = slice(b * BLK, (b + 1) * BLK)
            p = softmax_keys(jnp.where(same, scores, -1e30))
            pb = p.astype(BF)
            ds = score_grad(p, prob_grad)
            o_slots[h, rows, : q.shape[1]] = tn(pb, v).astype(BF)
            v_slots[h, rows, : q.shape[1]] = nn(pb, do).astype(BF)
            k_slots[h, rows, : q.shape[1]] = nn(ds, q).astype(BF)
            q_slots[h, rows, : q.shape[1]] = tn(ds, k).astype(BF)

    all_heads(head, rest)
    merge(o_slots, mix)
    out_copies = store_blocks(mix, mixed_hbm, io_sems, 4)
    dh[...] = project_back((q_slots, k_slots, v_slots), dqkv, wq).astype(BF)
    out_copies += store_blocks(dh, dhid_hbm, io_sems, 6)
    for copy in out_copies:
        copy.wait()


def spatial_backward(dhid_hbm, mix_hbm, gt, og_hbm, qkv_hbm, prob_hbm, video_hbm, gs,
                     wo_hbm, wq_hbm, out, dhid, mix, stream, og, qkv, prob, video, wo, wq,
                     sg, sgb, dmix, dqkv, dh, q_slots, k_slots, v_slots, sems):
    pairs = (
        (wo_hbm, wo), (mix_hbm, mix), (video_hbm, video), (dhid_hbm, dhid), (og_hbm, og),
        (qkv_hbm, qkv), (prob_hbm, prob), (wq_hbm, wq),
    )
    copies = [fetch(src, dst, sems.at[i]) for i, (src, dst) in enumerate(pairs)]
    for copy in copies[:3]:
        copy.wait()
    stream[...] = video[...].astype(F32) + nn(mix[...], wo[...])
    for copy in copies[3:5]:
        copy.wait()

    def stream_grad(rows):
        dx = norm_back(stream[rows, :], gt[...].reshape(1, D), dhid[rows, :].astype(F32))
        total = og[rows, :].astype(F32) + dx
        sg[rows, :] = total
        sgb[rows, :] = total.astype(BF)

    row_blocks(stream_grad)
    dmix[...] = nt(sgb[...], wo[...]).astype(BF)
    copies[5].wait()
    copies[6].wait()

    def head(h):
        low, width, inside = window(h)
        qs, ks, vs = pl.ds(low, width), pl.ds(D + low, width), pl.ds(2 * D + low, width)
        q = qkv[:, qs] * inside
        k = qkv[:, ks] * inside
        v = qkv[:, vs]
        do = dmix[:, qs] * inside
        return nt(v, do), q, k, do

    def rest(h, prob_grad, q, k, do):
        pb = prob[h]
        ds = score_grad(pb.astype(F32), prob_grad)
        v_slots[h, :, : q.shape[1]] = nn(pb, do).astype(BF)
        k_slots[h, :, : q.shape[1]] = nn(ds, q).astype(BF)
        q_slots[h, :, : q.shape[1]] = tn(ds, k).astype(BF)

    all_heads(head, rest)
    copies[7].wait()
    dh[...] = project_back((q_slots, k_slots, v_slots), dqkv, wq).astype(BF)

    def video_grad(rows):
        dx = norm_back(video[rows, :].astype(F32), gs[...].reshape(1, D), dh[rows, :].astype(F32))
        out[rows, :] = (sg[rows, :] + dx).astype(BF)

    row_blocks(video_grad)


GROUPS = DP // 2


SUB = 8


def outer_product(core, mixed, other_mixed, og, other_og, out, m, g, full, sems):
    copies = [
        fetch(mixed, m.at[:T, :], sems.at[0]),
        fetch(og, g.at[:T, :], sems.at[1]),
        fetch(other_mixed, m.at[T:, :], sems.at[2]),
        fetch(other_og, g.at[T:, :], sems.at[3]),
    ]
    for copy in copies:
        copy.wait()
    step = 3 * LANES
    for c in range(D // step):
        full[c * step : (c + 1) * step, :] = tn(m[:, c * step : (c + 1) * step], g[...])
    place = lax.broadcasted_iota(jnp.int32, (SUB, 1), 0)

    def body(i, carry):
        base = (2 * i + core[0]) * HD
        for j in range(SEQ):
            at = base + j * SUB
            upper = full[pl.ds(pl.multiple_of(at, SUB), SUB), :]
            lower = full[pl.ds(pl.multiple_of(at + SUB, SUB), SUB), :]
            eight = jnp.where(place >= j, upper, lower)
            ninth = lower[j : j + 1, :]
            parts = [eight[:, t * LANES : (t + 1) * LANES] for t in range(TILES)]
            for first in (0, SUB):
                rest = jnp.zeros((SUB, LANES), F32)
                for t in range(first, min(first + SUB, TILES)):
                    rest = jnp.where(
                        place == t - first, ninth[:, t * LANES : (t + 1) * LANES], rest
                    )
                parts.append(rest)
            out[i * SEQ + j] = jnp.concatenate(parts).astype(BF)
        return carry

    lax.fori_loop(0, GROUPS, body, 0)


def sum_chunks(owner, got_hbm, out, got, total, sems, *, scale):
    step = GROUPS * SEQ // 4
    pieces = [slice(i * step, (i + 1) * step) for i in range(4)]
    copies = [fetch(got_hbm.at[p], got.at[p], sems.at[i]) for i, p in enumerate(pieces)]
    for i, (copy, p) in enumerate(zip(copies, pieces)):
        copy.wait()
        part = jnp.sum(got[p].astype(F32), axis=0)
        total[...] = part if i == 0 else total[...] + part
    total[...] *= scale
    back = lax.rem(SUB - owner[0], SUB)
    for t in range(TILES):
        lanes = slice(t * LANES, (t + 1) * LANES)
        out[:SUB, lanes] = pltpu.roll(total[t * SUB : (t + 1) * SUB, :], back, 0)
        out[SUB:, lanes] = total[TILES * SUB + t : TILES * SUB + t + 1, :]


def call(fn, outs, args, scratch, flops, specs=None, out_specs=None):
    if specs is None:
        specs = [VMEM] * len(args)
    if out_specs is None:
        out_specs = [VMEM] * len(outs)
    moved = sum(a.size * a.dtype.itemsize for a in args)
    moved += sum(math.prod(s) * jnp.dtype(d).itemsize for s, d in outs)
    return pl.pallas_call(
        fn,
        out_shape=[jax.ShapeDtypeStruct(s, d) for s, d in outs],
        in_specs=[pl.BlockSpec(memory_space=s) for s in specs],
        out_specs=[pl.BlockSpec(memory_space=s) for s in out_specs],
        scratch_shapes=scratch,
        cost_estimate=pl.CostEstimate(flops=flops, bytes_accessed=moved, transcendentals=0),
    )(*args)


UNIT = 2 * T * D * D
WIDE, SQUARE = VMEM((D, 3 * D), BF), VMEM((D, D), BF)
TOK, TOK3, TOKF = VMEM((T, D), BF), VMEM((T, 3 * D), BF), VMEM((T, D), F32)
PROB, SLOTS = VMEM((HEADS, T, T), BF), VMEM((HEADS, T, WIN), BF)
DMA = pltpu.SemaphoreType.DMA


def run_spatial_forward(clip, gs, gt, wq, wo):
    return call(
        spatial_forward,
        [((T, D), BF), ((T, D), BF), ((T, 3 * D), BF), ((HEADS, T, T), BF)],
        (clip, gs, gt, wq, wo),
        [WIDE, SQUARE, TOK, TOK, TOKF, TOK3, PROB, SLOTS, DMA((5,)), DMA((5,))],
        5 * UNIT,
        [VMEM, VMEM, VMEM, ANY, ANY],
        [ANY, ANY, ANY, ANY],
    )


def run_temporal(hid, dmix, wq):
    return call(
        temporal,
        [((SEQ, POS, D), BF), ((SEQ, POS, D), BF)],
        (hid, dmix, wq),
        [WIDE, TOK, TOK, TOK3, TOK, TOK3, TOK, SLOTS, SLOTS, SLOTS, SLOTS, DMA((4,)),
         DMA((8,))],
        8 * UNIT,
        [ANY, ANY, ANY],
        [ANY, ANY],
    )


def run_spatial_backward(dhid, mix, gt, og, qkv, prob, clip, gs, wo, wq):
    return call(
        spatial_backward,
        [((T, D), BF)],
        (dhid, mix, gt, og, qkv, prob, clip, gs, wo, wq),
        [TOK, TOK, TOKF, TOK, TOK3, PROB, TOK, SQUARE, WIDE, TOKF, TOK, TOK, TOK3, TOK,
         SLOTS, SLOTS, SLOTS, DMA((8,))],
        7 * UNIT,
        [ANY, ANY, VMEM, ANY, ANY, ANY, ANY, VMEM, ANY, ANY],
    )[0]


def run_outer_product(core, mixed, other_mixed, og, other_og):
    pair = VMEM((2 * T, D), BF)
    return call(
        outer_product,
        [((GROUPS * SEQ, CHUNK, LANES), BF)],
        (core, mixed, other_mixed, og, other_og),
        [pair, pair, VMEM((D, D), F32), DMA((4,))],
        2 * UNIT,
        [pltpu.SMEM, ANY, ANY, ANY, ANY],
    )[0]


def run_sum_chunks(owner, parts, scale):
    def finish(*refs):
        sum_chunks(*refs, scale=scale)

    return call(
        finish,
        [((OWN, D), F32)],
        (owner, parts),
        [VMEM((GROUPS * SEQ, CHUNK, LANES), BF), VMEM((CHUNK, LANES), F32), DMA((4,))],
        1000,
        [pltpu.SMEM, ANY],
    )[0]


def per_device(
    video,
    out_grad,
    gain_spatial,
    gain_temporal,
    w_spatial_qkv,
    w_spatial_out,
    w_temporal_qkv,
    w_temporal_out,
):
    tokens = lax.axis_size("dp") * video.shape[0] * SEQ * T
    shape = video.shape
    clip = video.reshape(T, D)
    og = out_grad.reshape(T, D)

    def exchange(x):
        return lax.all_to_all(x.reshape(SEQ, POS, D), "seq", 0, 0, tiled=True)

    def swap(x):
        return lax.ppermute(x, "dp", [(i, i ^ 1) for i in range(DP)])

    og_pos = exchange(og)
    other_og = swap(og_pos)
    hid, mix, qkv, prob = run_spatial_forward(
        clip, gain_spatial, gain_temporal, w_spatial_qkv, w_spatial_out
    )
    hid_pos = exchange(hid)
    dmix = nt(og_pos.reshape(T, D), w_temporal_out).astype(BF).reshape(SEQ, POS, D)
    mixed_pos, dhid_pos = run_temporal(hid_pos, dmix, w_temporal_qkv)
    dhid = exchange(dhid_pos).reshape(T, D)

    core = lax.rem(lax.axis_index("dp"), 2).reshape(1)
    other_mixed = swap(mixed_pos)
    chunks = run_outer_product(
        core, *(x.reshape(T, D) for x in (mixed_pos, other_mixed, og_pos, other_og))
    )
    chunks, dhid = lax.optimization_barrier((chunks, dhid))
    owners = [
        [(g * 2 + c) * SEQ + s for g in range(GROUPS) for s in range(SEQ)] for c in range(2)
    ]
    parts = lax.all_to_all(
        chunks, ("dp", "seq"), 0, 0, axis_index_groups=owners, tiled=True
    )
    video_grad = run_spatial_backward(
        dhid, mix, gain_temporal, og, qkv, prob, clip, gain_spatial,
        w_spatial_out, w_spatial_qkv,
    )
    owner = lax.axis_index("seq").reshape(1)
    w_grad = run_sum_chunks(owner, parts, 1.0 / math.sqrt(float(tokens)))
    return (video_grad.reshape(shape), w_grad)


def solution(mesh):
    return jax.shard_map(
        per_device,
        mesh=mesh,
        in_specs=(
            P("dp", "seq", None, None),
            P("dp", "seq", None, None),
            P(),
            P(),
            P(),
            P(),
            P(),
            P(),
        ),
        out_specs=(P("dp", "seq", None, None), P(("dp", "seq"), None)),
        check_vma=False,
    )
```

```python
import math

import jax
import jax.numpy as jnp
from jax import lax
from jax.experimental import pallas as pl
from jax.experimental.pallas import tpu as pltpu
from jax.sharding import PartitionSpec as P


HEADS = 16
D = 1152
HD = D // HEADS
T = 256
SEQ = 8
POS = T // SEQ
DP = 16
EPS = 1e-06
LOG2E = 1.0 / math.log(2.0)
SCALE = 1.0 / math.sqrt(HD)
BF = jnp.bfloat16
F32 = jnp.float32
ROWS = 32
WIN = 256
CHUNK = 88
OWN = D // (DP * SEQ)
LANES = 128
TILES = D // LANES

VMEM = pltpu.VMEM
ANY = pl.ANY


def nn(a, b):
    return lax.dot_general(a, b, (((1,), (0,)), ((), ())), preferred_element_type=F32)


def nt(a, b):
    return lax.dot_general(a, b, (((1,), (1,)), ((), ())), preferred_element_type=F32)


def tn(a, b):
    return lax.dot_general(a, b, (((0,), (0,)), ((), ())), preferred_element_type=F32)


def row_stats(x):
    center = jnp.mean(x, axis=-1, keepdims=True)
    centered = x - center
    spread = jnp.mean(centered * centered, axis=-1, keepdims=True)
    return centered, lax.rsqrt(spread + EPS)


def row_blocks(fn, first=0, last=T // ROWS):
    def body(i, carry):
        fn(pl.ds(pl.multiple_of(i * ROWS, ROWS), ROWS))
        return carry

    lax.fori_loop(first, last, body, 0, unroll=4)


def norm_back(x, g, dy):
    centered, inv = row_stats(x)
    xhat = centered * inv
    dxhat = dy * g
    mean_d = jnp.mean(dxhat, axis=-1, keepdims=True)
    mean_dx = jnp.mean(dxhat * xhat, axis=-1, keepdims=True)
    return inv * (dxhat - mean_d - xhat * mean_dx)


def window(h):
    low = h * HD // LANES * LANES
    width = -(-(h * HD + HD - low) // LANES) * LANES
    start = h * HD - low
    lane = lax.broadcasted_iota(jnp.int32, (1, width), 1)
    inside = jnp.where((lane >= start) & (lane < start + HD), 1.0, 0.0)
    return low, width, inside.astype(BF)


def softmax_keys(scores):
    top = jnp.max(scores, axis=0, keepdims=True)
    e = jnp.exp2((scores - top) * (SCALE * LOG2E))
    return e * (1.0 / jnp.sum(e, axis=0, keepdims=True))


def score_grad(prob, prob_grad):
    t = prob * prob_grad
    delta = jnp.sum(t, axis=0, keepdims=True)
    return ((t - prob * delta) * SCALE).astype(BF)


def all_heads(first, second):
    waiting = []
    for h in range(HEADS):
        waiting.append((h, first(h)))
        if len(waiting) > 2:
            at, values = waiting.pop(0)
            second(at, *values)
    for at, values in waiting:
        second(at, *values)


def merge(slots, dst, base=0):
    for t in range(TILES):
        total = None
        for h in range(HEADS):
            if h * HD < (t + 1) * LANES and (h + 1) * HD > t * LANES:
                at = (t - h * HD // LANES) * LANES
                piece = slots[h, :, at : at + LANES]
                total = piece if total is None else total + piece
        dst[:, base + t * LANES : base + (t + 1) * LANES] = total


def project_back(slots, grad, weight):
    total = None
    for i, section in enumerate(slots):
        merge(section, grad, i * D)
        cols = slice(i * D, (i + 1) * D)
        part = nt(grad[:, cols], weight[:, cols])
        total = part if total is None else total + part
    return total


def fetch(src, dst, sem):
    copy = pltpu.make_async_copy(src, dst, sem)
    copy.start()
    return copy


CUTS = (0, 512, 1536, 2560, 3456)
PIECES = [slice(a, b) for a, b in zip(CUTS, CUTS[1:])]


def fetch_columns(src, dst, sems):
    return [fetch(src.at[:, p], dst.at[:, p], sems.at[i]) for i, p in enumerate(PIECES)]


def spatial_forward(video, gs, gt, wq_hbm, wo_hbm, hid_hbm, mix_hbm, qkv_hbm,
                    wq, wo, hid, mix, stream, qkv, slots, sems, out_sems):
    wq_copies = fetch_columns(wq_hbm, wq, sems)
    wo_copy = fetch(wo_hbm, wo, sems.at[4])

    def first_norm(rows):
        centered, inv = row_stats(video[rows, :].astype(F32))
        hid[rows, :] = (centered * inv * gs[...].reshape(1, D)).astype(BF)

    row_blocks(first_norm)
    for copy, p in zip(wq_copies, PIECES):
        copy.wait()
        qkv[:, p] = nn(hid[...], wq[:, p]).astype(BF)
    qkv_copy = fetch(qkv, qkv_hbm, out_sems.at[0])

    def head(h):
        low, width, inside = window(h)
        q = qkv[:, pl.ds(low, width)] * inside
        k = qkv[:, pl.ds(D + low, width)]
        v = qkv[:, pl.ds(2 * D + low, width)] * inside
        return nt(k, q), v

    def rest(h, scores, v):
        p = softmax_keys(scores).astype(BF)
        slots[h, :, : v.shape[1]] = tn(p, v).astype(BF)

    all_heads(head, rest)
    merge(slots, mix)
    mix_copy = fetch(mix, mix_hbm, out_sems.at[2])
    wo_copy.wait()
    stream[...] = video[...].astype(F32) + nn(mix[...], wo[...])

    def second_norm(rows):
        centered, inv = row_stats(stream[rows, :])
        hid[rows, :] = (centered * inv * gt[...].reshape(1, D)).astype(BF)

    copies = [qkv_copy, mix_copy]
    for i in range(2):
        row_blocks(second_norm, i * T // ROWS // 2, (i + 1) * T // ROWS // 2)
        rows = slice(i * T // 2, (i + 1) * T // 2)
        copies.append(fetch(hid.at[rows, :], hid_hbm.at[rows, :], out_sems.at[3 + i]))
    for copy in copies:
        copy.wait()


HALF = POS // 2
BLK = SEQ * HALF


def block_of(ref, b):
    return ref.at[b * BLK : (b + 1) * BLK, :].reshape(SEQ, HALF, D)


def fetch_blocks(src, dst, sems, first):
    return [
        fetch(src.at[:, b * HALF : (b + 1) * HALF, :], block_of(dst, b), sems.at[first + b])
        for b in range(2)
    ]


def store_blocks(src, dst, sems, first):
    return [
        fetch(block_of(src, b), dst.at[:, b * HALF : (b + 1) * HALF, :], sems.at[first + b])
        for b in range(2)
    ]


def temporal(hid_hbm, dmix_hbm, wq_hbm, mixed_hbm, dhid_hbm,
             wq, hid, dmix, qkv, mix, dqkv, dh, o_slots, q_slots, k_slots, v_slots, sems, io_sems):
    hid_copies = fetch_blocks(hid_hbm, hid, io_sems, 0)
    wq_copies = fetch_columns(wq_hbm, wq, sems)
    dmix_copies = fetch_blocks(dmix_hbm, dmix, io_sems, 2)
    for copy in hid_copies:
        copy.wait()
    for copy, p in zip(wq_copies, PIECES):
        copy.wait()
        qkv[:, p] = nn(hid[...], wq[:, p]).astype(BF)
    for copy in dmix_copies:
        copy.wait()

    key_pos = lax.rem(lax.broadcasted_iota(jnp.int32, (BLK, BLK), 0), HALF)
    query_pos = lax.rem(lax.broadcasted_iota(jnp.int32, (BLK, BLK), 1), HALF)
    same = key_pos == query_pos

    def head(h):
        low, width, inside = window(h)
        values = []
        for b in range(2):
            rows = slice(b * BLK, (b + 1) * BLK)
            qs, ks, vs = pl.ds(low, width), pl.ds(D + low, width), pl.ds(2 * D + low, width)
            q = qkv[rows, qs] * inside
            k = qkv[rows, ks] * inside
            v = qkv[rows, vs] * inside
            do = dmix[rows, qs] * inside
            values.append((nt(k, q), nt(v, do), q, k, v, do))
        return values

    def rest(h, *values):
        for b, (scores, prob_grad, q, k, v, do) in enumerate(values):
            rows = slice(b * BLK, (b + 1) * BLK)
            p = softmax_keys(jnp.where(same, scores, -1e30))
            pb = p.astype(BF)
            ds = score_grad(p, prob_grad)
            o_slots[h, rows, : q.shape[1]] = tn(pb, v).astype(BF)
            v_slots[h, rows, : q.shape[1]] = nn(pb, do).astype(BF)
            k_slots[h, rows, : q.shape[1]] = nn(ds, q).astype(BF)
            q_slots[h, rows, : q.shape[1]] = tn(ds, k).astype(BF)

    all_heads(head, rest)
    merge(o_slots, mix)
    out_copies = store_blocks(mix, mixed_hbm, io_sems, 4)
    dh[...] = project_back((q_slots, k_slots, v_slots), dqkv, wq).astype(BF)
    out_copies += store_blocks(dh, dhid_hbm, io_sems, 6)
    for copy in out_copies:
        copy.wait()


def spatial_backward(dhid_hbm, mix_hbm, gt, og_hbm, qkv_hbm, video_hbm, gs,
                     wo_hbm, wq_hbm, out, dhid, mix, stream, og, qkv, video, wo, wq,
                     sg, sgb, dmix, dqkv, dh, q_slots, k_slots, v_slots, sems):
    pairs = (
        (wo_hbm, wo), (mix_hbm, mix), (video_hbm, video), (dhid_hbm, dhid), (og_hbm, og),
        (qkv_hbm, qkv), (wq_hbm, wq),
    )
    copies = [fetch(src, dst, sems.at[i]) for i, (src, dst) in enumerate(pairs)]
    for copy in copies[:3]:
        copy.wait()
    stream[...] = video[...].astype(F32) + nn(mix[...], wo[...])
    for copy in copies[3:5]:
        copy.wait()

    def stream_grad(rows):
        dx = norm_back(stream[rows, :], gt[...].reshape(1, D), dhid[rows, :].astype(F32))
        total = og[rows, :].astype(F32) + dx
        sg[rows, :] = total
        sgb[rows, :] = total.astype(BF)

    row_blocks(stream_grad)
    dmix[...] = nt(sgb[...], wo[...]).astype(BF)
    copies[5].wait()

    def head(h):
        low, width, inside = window(h)
        qs, ks, vs = pl.ds(low, width), pl.ds(D + low, width), pl.ds(2 * D + low, width)
        q = qkv[:, qs] * inside
        k = qkv[:, ks] * inside
        v = qkv[:, vs]
        do = dmix[:, qs] * inside
        return nt(k, q), nt(v, do), q, k, do

    def rest(h, scores, prob_grad, q, k, do):
        p = softmax_keys(scores)
        pb = p.astype(BF)
        ds = score_grad(p, prob_grad)
        v_slots[h, :, : q.shape[1]] = nn(pb, do).astype(BF)
        k_slots[h, :, : q.shape[1]] = nn(ds, q).astype(BF)
        q_slots[h, :, : q.shape[1]] = tn(ds, k).astype(BF)

    all_heads(head, rest)
    copies[6].wait()
    dh[...] = project_back((q_slots, k_slots, v_slots), dqkv, wq).astype(BF)

    def video_grad(rows):
        dx = norm_back(video[rows, :].astype(F32), gs[...].reshape(1, D), dh[rows, :].astype(F32))
        out[rows, :] = (sg[rows, :] + dx).astype(BF)

    row_blocks(video_grad)


GROUPS = DP // 2


SUB = 8


def outer_product(core, mixed, other_mixed, og, other_og, out, m, g, full, sems):
    copies = [
        fetch(mixed, m.at[:T, :], sems.at[0]),
        fetch(og, g.at[:T, :], sems.at[1]),
        fetch(other_mixed, m.at[T:, :], sems.at[2]),
        fetch(other_og, g.at[T:, :], sems.at[3]),
    ]
    for copy in copies:
        copy.wait()
    step = 3 * LANES
    for c in range(D // step):
        full[c * step : (c + 1) * step, :] = tn(m[:, c * step : (c + 1) * step], g[...])
    place = lax.broadcasted_iota(jnp.int32, (SUB, 1), 0)

    def body(i, carry):
        base = (2 * i + core[0]) * HD
        for j in range(SEQ):
            at = base + j * SUB
            upper = full[pl.ds(pl.multiple_of(at, SUB), SUB), :]
            lower = full[pl.ds(pl.multiple_of(at + SUB, SUB), SUB), :]
            eight = jnp.where(place >= j, upper, lower)
            ninth = lower[j : j + 1, :]
            parts = [eight[:, t * LANES : (t + 1) * LANES] for t in range(TILES)]
            for first in (0, SUB):
                rest = jnp.zeros((SUB, LANES), F32)
                for t in range(first, min(first + SUB, TILES)):
                    rest = jnp.where(
                        place == t - first, ninth[:, t * LANES : (t + 1) * LANES], rest
                    )
                parts.append(rest)
            out[i * SEQ + j] = jnp.concatenate(parts).astype(BF)
        return carry

    lax.fori_loop(0, GROUPS, body, 0)


def sum_chunks(owner, got_hbm, out, got, total, sems, *, scale):
    step = GROUPS * SEQ // 4
    pieces = [slice(i * step, (i + 1) * step) for i in range(4)]
    copies = [fetch(got_hbm.at[p], got.at[p], sems.at[i]) for i, p in enumerate(pieces)]
    for i, (copy, p) in enumerate(zip(copies, pieces)):
        copy.wait()
        part = jnp.sum(got[p].astype(F32), axis=0)
        total[...] = part if i == 0 else total[...] + part
    total[...] *= scale
    back = lax.rem(SUB - owner[0], SUB)
    for t in range(TILES):
        lanes = slice(t * LANES, (t + 1) * LANES)
        out[:SUB, lanes] = pltpu.roll(total[t * SUB : (t + 1) * SUB, :], back, 0)
        out[SUB:, lanes] = total[TILES * SUB + t : TILES * SUB + t + 1, :]


def call(fn, outs, args, scratch, flops, specs=None, out_specs=None):
    if specs is None:
        specs = [VMEM] * len(args)
    if out_specs is None:
        out_specs = [VMEM] * len(outs)
    moved = sum(a.size * a.dtype.itemsize for a in args)
    moved += sum(math.prod(s) * jnp.dtype(d).itemsize for s, d in outs)
    return pl.pallas_call(
        fn,
        out_shape=[jax.ShapeDtypeStruct(s, d) for s, d in outs],
        in_specs=[pl.BlockSpec(memory_space=s) for s in specs],
        out_specs=[pl.BlockSpec(memory_space=s) for s in out_specs],
        scratch_shapes=scratch,
        cost_estimate=pl.CostEstimate(flops=flops, bytes_accessed=moved, transcendentals=0),
    )(*args)


UNIT = 2 * T * D * D
WIDE, SQUARE = VMEM((D, 3 * D), BF), VMEM((D, D), BF)
TOK, TOK3, TOKF = VMEM((T, D), BF), VMEM((T, 3 * D), BF), VMEM((T, D), F32)
SLOTS = VMEM((HEADS, T, WIN), BF)
DMA = pltpu.SemaphoreType.DMA


def run_spatial_forward(clip, gs, gt, wq, wo):
    return call(
        spatial_forward,
        [((T, D), BF), ((T, D), BF), ((T, 3 * D), BF)],
        (clip, gs, gt, wq, wo),
        [WIDE, SQUARE, TOK, TOK, TOKF, TOK3, SLOTS, DMA((5,)), DMA((5,))],
        5 * UNIT,
        [VMEM, VMEM, VMEM, ANY, ANY],
        [ANY, ANY, ANY],
    )


def run_temporal(hid, dmix, wq):
    return call(
        temporal,
        [((SEQ, POS, D), BF), ((SEQ, POS, D), BF)],
        (hid, dmix, wq),
        [WIDE, TOK, TOK, TOK3, TOK, TOK3, TOK, SLOTS, SLOTS, SLOTS, SLOTS, DMA((4,)),
         DMA((8,))],
        8 * UNIT,
        [ANY, ANY, ANY],
        [ANY, ANY],
    )


def run_spatial_backward(dhid, mix, gt, og, qkv, clip, gs, wo, wq):
    return call(
        spatial_backward,
        [((T, D), BF)],
        (dhid, mix, gt, og, qkv, clip, gs, wo, wq),
        [TOK, TOK, TOKF, TOK, TOK3, TOK, SQUARE, WIDE, TOKF, TOK, TOK, TOK3, TOK,
         SLOTS, SLOTS, SLOTS, DMA((7,))],
        7 * UNIT,
        [ANY, ANY, VMEM, ANY, ANY, ANY, VMEM, ANY, ANY],
    )[0]


def run_outer_product(core, mixed, other_mixed, og, other_og):
    pair = VMEM((2 * T, D), BF)
    return call(
        outer_product,
        [((GROUPS * SEQ, CHUNK, LANES), BF)],
        (core, mixed, other_mixed, og, other_og),
        [pair, pair, VMEM((D, D), F32), DMA((4,))],
        2 * UNIT,
        [pltpu.SMEM, ANY, ANY, ANY, ANY],
    )[0]


def run_sum_chunks(owner, parts, scale):
    def finish(*refs):
        sum_chunks(*refs, scale=scale)

    return call(
        finish,
        [((OWN, D), F32)],
        (owner, parts),
        [VMEM((GROUPS * SEQ, CHUNK, LANES), BF), VMEM((CHUNK, LANES), F32), DMA((4,))],
        1000,
        [pltpu.SMEM, ANY],
    )[0]


def per_device(
    video,
    out_grad,
    gain_spatial,
    gain_temporal,
    w_spatial_qkv,
    w_spatial_out,
    w_temporal_qkv,
    w_temporal_out,
):
    tokens = lax.axis_size("dp") * video.shape[0] * SEQ * T
    shape = video.shape
    clip = video.reshape(T, D)
    og = out_grad.reshape(T, D)

    def exchange(x):
        return lax.all_to_all(x.reshape(SEQ, POS, D), "seq", 0, 0, tiled=True)

    def swap(x):
        return lax.ppermute(x, "dp", [(i, i ^ 1) for i in range(DP)])

    og_pos = exchange(og)
    other_og = swap(og_pos)
    hid, mix, qkv = run_spatial_forward(
        clip, gain_spatial, gain_temporal, w_spatial_qkv, w_spatial_out
    )
    hid_pos = exchange(hid)
    dmix = nt(og_pos.reshape(T, D), w_temporal_out).astype(BF).reshape(SEQ, POS, D)
    mixed_pos, dhid_pos = run_temporal(hid_pos, dmix, w_temporal_qkv)
    dhid = exchange(dhid_pos).reshape(T, D)

    core = lax.rem(lax.axis_index("dp"), 2).reshape(1)
    other_mixed = swap(mixed_pos)
    chunks = run_outer_product(
        core, *(x.reshape(T, D) for x in (mixed_pos, other_mixed, og_pos, other_og))
    )
    chunks, dhid = lax.optimization_barrier((chunks, dhid))
    owners = [
        [(g * 2 + c) * SEQ + s for g in range(GROUPS) for s in range(SEQ)] for c in range(2)
    ]
    parts = lax.all_to_all(
        chunks, ("dp", "seq"), 0, 0, axis_index_groups=owners, tiled=True
    )
    video_grad = run_spatial_backward(
        dhid, mix, gain_temporal, og, qkv, clip, gain_spatial,
        w_spatial_out, w_spatial_qkv,
    )
    owner = lax.axis_index("seq").reshape(1)
    w_grad = run_sum_chunks(owner, parts, 1.0 / math.sqrt(float(tokens)))
    return (video_grad.reshape(shape), w_grad)


def solution(mesh):
    return jax.shard_map(
        per_device,
        mesh=mesh,
        in_specs=(
            P("dp", "seq", None, None),
            P("dp", "seq", None, None),
            P(),
            P(),
            P(),
            P(),
            P(),
            P(),
        ),
        out_specs=(P("dp", "seq", None, None), P(("dp", "seq"), None)),
        check_vma=False,
    )
```
